256 devices in a mesh: seq: 64 (over y, z_hi, x, core), adapter: 4 (over z_lo).
Axes of the slice: x: 4, y: 4, z: 8 (z_hi: 2, z_lo: 4; z = z_hi * 4 + z_lo), core: 2. Of those that a mesh axis runs over, the one named last changes fastest.
Arguments:
- hidden: bfloat16 [8, 8192, 8192], P('adapter', 'seq'), may hold values from -6 to 6
- response_base_queries: bfloat16 [8, 8192, 1024], P('adapter', 'seq'), may hold values from -6 to 6
- attention_output_gradient: bfloat16 [8, 8192, 1024], P('adapter', 'seq'), may hold values from -6 to 6
- keys: bfloat16 [49152, 128], P('seq'), may hold values from -6 to 6
- values: bfloat16 [49152, 128], P('seq'), may hold values from -6 to 6
- adapter_down_weight: bfloat16 [8, 16, 8192], P('adapter'), may hold values from -0.0625 to 0.0625
- adapter_up_weight: bfloat16 [8, 16, 1024], P('adapter'), may hold values from -1.5 to 1.5
- lengths: int32 [8], P('adapter'), may hold values from 4096 to 8192
- offsets: int32 [8, 8192], P('adapter', 'seq'), may hold values from 0 to 49151, as said below
Outputs:
- adapter_down_gradient: float32 [8, 16, 8192], P('adapter', None, 'seq')
- adapter_up_gradient: float32 [8, 16, 1024], P('adapter')
- prompt_key_gradient: float32 [49152, 128], P(('seq', 'adapter'))
- prompt_value_gradient: float32 [49152, 128], P(('seq', 'adapter'))
The draws below stay inside these ranges and needn't reach their ends.
Inputs may be any that keep to these rules, and one draw needn't show every extreme that they name: Row r of every adapter has offsets in [(r // 128) * 768, (r // 128 + 1) * 768).
All inputs are finite; a program needn't handle non-finite values.
Results may differ from the reference program's by a relative error of at most 0.025.
The reference program's roundings to bfloat16 on the way count: a program that leaves them out, or rounds other values in their place, can miss the bound.
Values may be sent and summed in bfloat16 or wider, within the bound.
No kernel may reach another device: no remote copies, remote signals or barrier semaphores. Data moves between devices by JAX's collectives and lax.ppermute only.
A program may use at most 192 MiB of HBM per device.

```python
import jax
import jax.numpy as jnp
from jax import lax

MODEL_WIDTH = 8192
GROUP = 8
HD = 128
ADAPTER_RANK = 16
PROMPT_SPAN = 768
RESP_DEV = 128
GROUP_FEATURES = 1024
SPAN = 2304
ADAPTER_COUNT = 8
PROMPT = 49152
RESP = 8192
N_SEQ = 64


def draw_keys(key, part):
    drawn = jnp.clip(jax.random.normal(jax.random.fold_in(key, 11), (PROMPT, HD), jnp.float32), -6.0, 6.0)
    return drawn.astype(jnp.bfloat16)


def draw_response_base_queries(key, part):
    drawn = jnp.clip(jax.random.normal(jax.random.fold_in(key, 13), (ADAPTER_COUNT, RESP, GROUP_FEATURES), jnp.float32), -6.0, 6.0)
    return drawn.astype(jnp.bfloat16)


def draw_offsets(key, part):
    inside = jax.random.randint(key, (ADAPTER_COUNT, RESP), 0, PROMPT_SPAN)
    anchor = jnp.arange(RESP, dtype=jnp.int32) // RESP_DEV * PROMPT_SPAN
    return (inside + anchor[None, :]).astype(jnp.int32)


def with_ends(array, own_key, smallest, top_value):
    shape = array.shape
    place = [jax.random.randint(jax.random.fold_in(own_key, axis), (), 0, shape[axis]) for axis in range(len(shape))]
    array = array.at[tuple(place)].set(smallest)
    longest = shape.index(max(shape))
    place[longest] = (place[longest] + 1) % shape[longest]
    return array.at[tuple(place)].set(top_value)


def level_of(rng, extent, shards, low, high):
    def one(position, blocks):
        steps = jax.random.uniform(jax.random.fold_in(jax.random.fold_in(rng, 6), position), (blocks,), jnp.float32, low / len(shards), high / len(shards))
        return jnp.repeat(jnp.exp(steps), extent[position] // blocks).reshape((-1,) + (1,) * (len(extent) - position - 1))

    factor_of = one(*shards[0])
    for cut in shards[1:]:
        factor_of = factor_of * one(*cut)
    return factor_of


def normal_values(rng, shape, deviation, limit, cuts=(), kind=jnp.bfloat16):
    result = deviation * jax.random.normal(rng, shape, jnp.float32)
    if cuts:
        result = result * level_of(rng, shape, cuts, -0.22, 0.18)
    return jnp.clip(result, -limit, limit).astype(kind)


def setup_inputs(seed: int = 0) -> dict:
    key_list = jax.random.split(jax.random.key(seed), 10)
    return {
        "hidden": normal_values(key_list[0], (ADAPTER_COUNT, RESP, MODEL_WIDTH), 1.0, 6.0, ((0, 4), (1, 64))),
        "response_base_queries": draw_response_base_queries(jax.random.fold_in(key_list[9], 71), 0),
        "attention_output_gradient": normal_values(key_list[2], (ADAPTER_COUNT, RESP, GROUP_FEATURES), 1.0, 6.0, ((0, 4), (1, 64))),
        "keys": draw_keys(jax.random.fold_in(key_list[9], 71), 0),
        "values": normal_values(key_list[4], (PROMPT, HD), 1.0, 6.0, ((0, 64),)),
        "adapter_down_weight": normal_values(key_list[5], (ADAPTER_COUNT, ADAPTER_RANK, MODEL_WIDTH), MODEL_WIDTH ** -0.5, 0.0625, ((0, 4),)),
        "adapter_up_weight": normal_values(key_list[6], (ADAPTER_COUNT, ADAPTER_RANK, GROUP_FEATURES), ADAPTER_RANK ** -0.5, 1.5, ((0, 4),)),
        "lengths": with_ends(jax.random.randint(key_list[7], (ADAPTER_COUNT,), RESP // 2, RESP + 1), jax.random.fold_in(key_list[7], 1), RESP // 2, RESP).astype(jnp.int32),
        "offsets": draw_offsets(jax.random.fold_in(key_list[9], 71), 0),
    }


adapter_scale = 2.0
masked_score = -1.0e30


def block_grads(query_blk, grad_blk, place_blk, key_win, value_win, first_pos):
    adapt_n, row_n, _ = query_blk.shape
    head_dim = key_win.shape[1]
    factor = head_dim ** -0.5
    query_heads = query_blk.reshape(adapt_n, row_n, GROUP, head_dim).astype(jnp.float32)
    grad_heads = grad_blk.reshape(adapt_n, row_n, GROUP, head_dim).astype(jnp.float32)
    key_pos = first_pos + jnp.arange(key_win.shape[0], dtype=jnp.int32)
    allowed = (key_pos[None, None, :] >= 0) & (key_pos[None, None, :] <= place_blk[:, :, None]) & (key_pos[None, None, :] > place_blk[:, :, None] - SPAN)
    allowed = allowed[:, :, None, :]
    scores = jnp.einsum("arhd,kd->arhk", query_heads, key_win.astype(jnp.float32)) * factor
    scores = jnp.where(allowed, scores, masked_score)
    peak_val = jnp.max(scores, axis=-1, keepdims=True)
    raised = jnp.exp(scores - peak_val)
    attn_prob = raised / jnp.sum(raised, axis=-1, keepdims=True)
    dprob = jnp.einsum("arhd,kd->arhk", grad_heads, value_win.astype(jnp.float32))
    delta = jnp.sum(attn_prob * dprob, axis=-1, keepdims=True)
    dscore = (attn_prob * (dprob - delta)).astype(jnp.bfloat16).astype(jnp.float32)
    prob_low = attn_prob.astype(jnp.bfloat16).astype(jnp.float32)
    value_part = jnp.einsum("arhk,arhd->kd", prob_low, grad_heads)
    key_part = jnp.einsum("arhk,arhd->kd", dscore, query_heads) * factor
    query_part = jnp.einsum("arhk,kd->arhd", dscore, key_win.astype(jnp.float32)) * factor
    return query_part.reshape(adapt_n, row_n, GROUP * head_dim), key_part, value_part


def reference(hidden, response_base_queries, attention_output_gradient, keys, values, adapter_down_weight, adapter_up_weight, lengths, offsets):
    def reduced_features_for(entry_tuple):
        input_matrix, a_mat, b_mat, base_matrix = entry_tuple
        reduced_matrix = jnp.dot(input_matrix, a_mat.T, preferred_element_type=jnp.float32).astype(jnp.bfloat16)
        upper_limit = jnp.dot(reduced_matrix, b_mat, preferred_element_type=jnp.float32)
        return reduced_matrix, (base_matrix.astype(jnp.float32) + adapter_scale * upper_limit).astype(jnp.bfloat16)

    reduced_features, query_rows = lax.map(reduced_features_for, (hidden, adapter_down_weight, adapter_up_weight, response_base_queries))
    row_index = jnp.arange(RESP, dtype=jnp.int32)
    live_rows = row_index[None, :] < lengths[:, None]
    grad_use = jnp.where(live_rows[:, :, None], attention_output_gradient, jnp.zeros_like(attention_output_gradient))
    query_blocks = query_rows.reshape(ADAPTER_COUNT, N_SEQ, RESP_DEV, GROUP_FEATURES).transpose(1, 0, 2, 3)
    grad_blocks = grad_use.reshape(ADAPTER_COUNT, N_SEQ, RESP_DEV, GROUP_FEATURES).transpose(1, 0, 2, 3)
    place_blocks = offsets.reshape(ADAPTER_COUNT, N_SEQ, RESP_DEV).transpose(1, 0, 2)
    leading = jnp.zeros((3 * PROMPT_SPAN, HD), jnp.bfloat16)
    keys_pad = jnp.concatenate([leading, keys], axis=0)
    values_pad = jnp.concatenate([leading, values], axis=0)
    zero_acc = jnp.zeros((PROMPT + 3 * PROMPT_SPAN, HD), jnp.float32)

    def scan_step(carry, entry_tuple):
        key_running_sum, value_running_sum = carry
        block_id, query_blk, grad_blk, place_blk = entry_tuple
        begin = (block_id * PROMPT_SPAN).astype(jnp.int32)
        key_win = lax.dynamic_slice(keys_pad, (begin, jnp.int32(0)), (4 * PROMPT_SPAN, HD))
        value_win = lax.dynamic_slice(values_pad, (begin, jnp.int32(0)), (4 * PROMPT_SPAN, HD))
        query_part, key_part, value_part = block_grads(query_blk, grad_blk, place_blk, key_win, value_win, begin - 3 * PROMPT_SPAN)
        key_old = lax.dynamic_slice(key_running_sum, (begin, jnp.int32(0)), (4 * PROMPT_SPAN, HD))
        value_old = lax.dynamic_slice(value_running_sum, (begin, jnp.int32(0)), (4 * PROMPT_SPAN, HD))
        key_running_sum = lax.dynamic_update_slice(key_running_sum, key_old + key_part, (begin, jnp.int32(0)))
        value_running_sum = lax.dynamic_update_slice(value_running_sum, value_old + value_part, (begin, jnp.int32(0)))
        return (key_running_sum, value_running_sum), query_part

    block_ids = jnp.arange(N_SEQ, dtype=jnp.int32)
    (key_running_sum, value_running_sum), query_parts = lax.scan(scan_step, (zero_acc, zero_acc), (block_ids, query_blocks, grad_blocks, place_blocks))
    query_gradient = query_parts.transpose(1, 0, 2, 3).reshape(ADAPTER_COUNT, RESP, GROUP_FEATURES).astype(jnp.bfloat16)

    def adapter_gradients(entry_tuple):
        input_matrix, reduced_matrix, query_grad_matrix, b_mat = entry_tuple
        up_gradient = adapter_scale * jnp.dot(reduced_matrix.T, query_grad_matrix, preferred_element_type=jnp.float32)
        reduced_gradient = jnp.dot(query_grad_matrix, b_mat.T, preferred_element_type=jnp.float32).astype(jnp.bfloat16)
        down_gradient = adapter_scale * jnp.dot(reduced_gradient.T, input_matrix, preferred_element_type=jnp.float32)
        return down_gradient, up_gradient

    adapter_down_gradient, adapter_up_gradient = lax.map(adapter_gradients, (hidden, reduced_features, query_gradient, adapter_up_weight))
    return adapter_down_gradient, adapter_up_gradient, key_running_sum[3 * PROMPT_SPAN:], value_running_sum[3 * PROMPT_SPAN:]
```

```python
import functools

import jax
import jax.numpy as jnp
from jax import lax
from jax.experimental import pallas as pl
from jax.experimental.pallas import tpu as pltpu
from jax.sharding import PartitionSpec as P

adapter_scale = 2.0
masked_score = -1.0e30
log2_e = 1.4426950408889634
both_axes = ("seq", "adapter")
row_n_seq = 8

NN = ((1,), (0,))
NT = ((1,), (1,))


def dot(a, b, dims):
    return lax.dot_general(a, b, (dims, ((), ())), preferred_element_type=jnp.float32)


def moved(value, by_even, by_odd):
    peers, planes = lax.axis_size("seq"), lax.axis_size("adapter")
    pairs = []
    for s in range(peers):
        t = s + (by_odd if s % 2 else by_even)
        if 0 <= t < peers:
            for a in range(planes):
                b = a if t // row_n_seq == s // row_n_seq else planes - 1 - a
                pairs.append((s * planes + a, t * planes + b))
    return lax.ppermute(value, both_axes, pairs)


def grouped(value, groups):
    return lax.all_to_all(value, "seq", 0, 0, axis_index_groups=groups, tiled=True)


def attention_kernel(
    where_ref, rel_ref, base_ref, grad_ref, low_ref, up_ref, kv_own, kv_mid, kv_far, kv_swap,
    dquery_ref, own_ref, mid_ref, far_ref, swap_ref,
    window, key_t, score, dprob, dscore_low, acc,
    *, stretch, chunk, rows, adapters, head_dim, heads,
):
    head = pl.program_id(0)
    factor = head_dim**-0.5
    shift = factor * log2_e
    parts = stretch // chunk
    wide = rows * adapters
    block = where_ref[0]
    odd = lax.rem(block, 2) == 1
    spans = [slice(d * stretch, (d + 1) * stretch) for d in range(4)]

    @pl.when(head == 0)
    def _():
        acc[...] = jnp.zeros_like(acc)
        window[spans[0], :] = kv_own[...]
        window[spans[2], :] = kv_mid[...]

        @pl.when(odd)
        def _():
            window[spans[1], :] = kv_far[...]
            window[spans[3], :] = kv_swap[...]

        @pl.when(jnp.logical_not(odd))
        def _():
            window[spans[1], :] = kv_swap[...]
            window[spans[3], :] = kv_far[...]

        for span in spans:
            key_t[:, span] = window[span, :head_dim].T

    query_list = []
    grad_list = []
    line = block * rows + lax.broadcasted_iota(jnp.int32, (rows, head_dim), 0)
    for a in range(adapters):
        raised = dot(low_ref[a], up_ref[a], NN)
        query_list.append(
            (base_ref[a].astype(jnp.float32) + adapter_scale * raised).astype(jnp.bfloat16)
        )
        live = line < where_ref[1 + a]
        grad_list.append(
            jnp.where(live, grad_ref[a].astype(jnp.float32), 0.0).astype(jnp.bfloat16)
        )
    query = jnp.concatenate(query_list, axis=0)
    grad = jnp.concatenate(grad_list, axis=0)
    rel = rel_ref[...]
    place = lax.broadcasted_iota(jnp.int32, (chunk, wide), 0)
    bias3 = jnp.where(block >= 3, 0.0, masked_score)

    def fold(x, op):
        return op(x.reshape(x.shape[0] // 8, 8, x.shape[1]), axis=0)

    peak = None
    for d in range(3):
        high = None
        for c in range(parts):
            at = slice(d * stretch + c * chunk, d * stretch + (c + 1) * chunk)
            s = dot(window[at, :head_dim], query, NT)
            dp = dot(window[at, head_dim:], grad, NT)
            if d == 0:
                early = rel >= place + c * chunk
                far = slice(3 * stretch + c * chunk, 3 * stretch + (c + 1) * chunk)
                s = jnp.where(early, s, dot(window[far, :head_dim], query, NT) + bias3)
                dp = jnp.where(early, dp, dot(window[far, head_dim:], grad, NT))
            score[at, :] = s
            dprob[at, :] = dp
            top = fold(s, jnp.max)
            high = top if high is None else jnp.maximum(high, top)
        if d:
            high = jnp.where(block >= d, high, masked_score)
        peak = high if peak is None else jnp.maximum(peak, high)
    peak = jnp.max(peak, axis=0, keepdims=True)
    total = jnp.zeros((8, wide), jnp.float32)
    delta = jnp.zeros((8, wide), jnp.float32)
    for d in range(3):
        level = peak if d == 0 else jnp.where(block >= d, peak, -masked_score)
        for c in range(parts):
            at = slice(d * stretch + c * chunk, d * stretch + (c + 1) * chunk)
            e = jnp.exp2((score[at, :] - level) * shift)
            score[at, :] = e
            total = total + fold(e, jnp.sum)
            delta = delta + fold(e * dprob[at, :], jnp.sum)
    scale = 1.0 / jnp.sum(total, axis=0, keepdims=True)
    delta = jnp.sum(delta, axis=0, keepdims=True) * scale
    zero = jnp.zeros((chunk, wide), jnp.float32)
    for d in range(3):
        for c in range(parts):
            at = slice(d * stretch + c * chunk, d * stretch + (c + 1) * chunk)
            p = score[at, :] * scale
            ds = p * (dprob[at, :] - delta)
            if d == 0:
                early = rel >= place + c * chunk
                pieces = (
                    (0, jnp.where(early, p, zero), jnp.where(early, ds, zero)),
                    (3, jnp.where(early, zero, p), jnp.where(early, zero, ds)),
                )
            else:
                pieces = ((d, p, ds),)
            for e, p_e, ds_e in pieces:
                to = slice(e * stretch + c * chunk, e * stretch + (c + 1) * chunk)
                p_e = p_e.astype(jnp.bfloat16)
                ds_e = ds_e.astype(jnp.bfloat16)
                dscore_low[to, :] = ds_e
                acc[to, :head_dim] += dot(ds_e, query, NN)
                acc[to, head_dim:] += dot(p_e, grad, NN)
    dquery = (dot(key_t[...], dscore_low[...], NN).T * factor).astype(jnp.bfloat16)
    for a in range(adapters):
        dquery_ref[a] = dquery[a * rows : (a + 1) * rows]

    @pl.when(head == heads - 1)
    def _():
        def put(out, span):
            out[:, :head_dim] = (acc[span, :head_dim] * factor).astype(out.dtype)
            out[:, head_dim:] = acc[span, head_dim:].astype(out.dtype)

        put(own_ref, spans[0])
        put(mid_ref, spans[2])

        @pl.when(odd)
        def _():
            put(far_ref, spans[1])
            put(swap_ref, spans[3])

        @pl.when(jnp.logical_not(odd))
        def _():
            put(far_ref, spans[3])
            put(swap_ref, spans[1])


def attention_grads(where, rel, base, grad, low, up, own, mid, far, swap):
    adapters, rows, features = base.shape
    stretch, both = own.shape
    head_dim = both // 2
    heads = features // head_dim
    rank = low.shape[2]
    wide = rows * adapters
    body = functools.partial(
        attention_kernel,
        stretch=stretch,
        chunk=256,
        rows=rows,
        adapters=adapters,
        head_dim=head_dim,
        heads=heads,
    )
    per_head = pl.BlockSpec((adapters, rows, head_dim), lambda h, w: (0, 0, h))

    def whole(*shape):
        return pl.BlockSpec(shape, lambda h, w: (0,) * len(shape))

    return pl.pallas_call(
        body,
        grid_spec=pltpu.PrefetchScalarGridSpec(
            num_scalar_prefetch=1,
            grid=(heads,),
            in_specs=[
                whole(1, wide),
                per_head,
                per_head,
                whole(adapters, rows, rank),
                pl.BlockSpec((adapters, rank, head_dim), lambda h, w: (0, 0, h)),
            ]
            + [whole(stretch, both)] * 4,
            out_specs=[per_head] + [whole(stretch, both)] * 4,
            scratch_shapes=[
                pltpu.VMEM((4 * stretch, both), jnp.bfloat16),
                pltpu.VMEM((head_dim, 4 * stretch), jnp.bfloat16),
                pltpu.VMEM((3 * stretch, wide), jnp.float32),
                pltpu.VMEM((3 * stretch, wide), jnp.float32),
                pltpu.VMEM((4 * stretch, wide), jnp.bfloat16),
                pltpu.VMEM((4 * stretch, both), jnp.float32),
            ],
        ),
        out_shape=[
            jax.ShapeDtypeStruct(base.shape, jnp.bfloat16),
            jax.ShapeDtypeStruct((stretch, both), jnp.float32),
            jax.ShapeDtypeStruct((stretch, both), jnp.float32),
            jax.ShapeDtypeStruct((stretch, both), jnp.bfloat16),
            jax.ShapeDtypeStruct((stretch, both), jnp.bfloat16),
        ],
        compiler_params=pltpu.CompilerParams(
            dimension_semantics=("arbitrary",), vmem_limit_bytes=44 * 1024 * 1024
        ),
        name="attention_grads",
    )(where, rel, base, grad, low, up, own, mid, far, swap)


def adapter_kernel(dquery_ref, low_ref, up_ref, hidden_ref, out_ref, small, *, adapters, rank, lanes, inner):
    step = pl.program_id(0)
    outer = pl.num_programs(0)

    @pl.when(step == 0)
    def _():
        for a in range(adapters):
            at = slice(a * rank, (a + 1) * rank)
            small[at, :] = dot(up_ref[a], dquery_ref[a], NT).astype(jnp.bfloat16)
            low_t = low_ref[a].astype(jnp.float32).T.astype(jnp.bfloat16)
            piece = adapter_scale * dot(low_t, dquery_ref[a], NN)
            for i in range(inner):
                out_ref[i, outer, at, :] = piece[:, i * lanes : (i + 1) * lanes].astype(out_ref.dtype)

    for a in range(adapters):
        at = slice(a * rank, (a + 1) * rank)
        piece = adapter_scale * dot(small[at, :], hidden_ref[a], NN)
        for i in range(inner):
            out_ref[i, step, at, :] = piece[:, i * lanes : (i + 1) * lanes].astype(out_ref.dtype)


def adapter_grads(dquery, low, up, hidden, inner, outer):
    adapters, rows, features = dquery.shape
    rank = low.shape[2]
    width = hidden.shape[2]
    lanes = width // (inner * outer)

    def whole(*shape):
        return pl.BlockSpec(shape, lambda g: (0,) * len(shape))

    return pl.pallas_call(
        functools.partial(adapter_kernel, adapters=adapters, rank=rank, lanes=lanes, inner=inner),
        grid=(outer,),
        in_specs=[
            whole(adapters, rows, features),
            whole(adapters, rows, rank),
            whole(adapters, rank, features),
            pl.BlockSpec((adapters, rows, inner * lanes), lambda g: (0, 0, g)),
        ],
        out_specs=whole(inner, outer + 1, adapters * rank, lanes),
        out_shape=jax.ShapeDtypeStruct((inner, outer + 1, adapters * rank, lanes), jnp.bfloat16),
        scratch_shapes=[pltpu.VMEM((adapters * rank, rows), jnp.bfloat16)],
        compiler_params=pltpu.CompilerParams(
            dimension_semantics=("arbitrary",), vmem_limit_bytes=24 * 1024 * 1024
        ),
        name="adapter_grads",
    )(dquery, low, up, hidden)


def local(
    hidden,
    response_base_queries,
    attention_output_gradient,
    keys,
    values,
    adapter_down_weight,
    adapter_up_weight,
    lengths,
    offsets,
):
    adapt_n, row_n, feature_n = response_base_queries.shape
    rank = adapter_down_weight.shape[1]
    stretch_n, head_dim = keys.shape
    seq_index = lax.axis_index("seq")
    planes = lax.axis_size("adapter")
    inner = row_n_seq
    outer = lax.axis_size("seq") // inner

    own = jnp.concatenate([keys, values], axis=1)
    mid = moved(own, 2, 2)
    far = moved(own, 1, 3)
    swap = moved(mid, 1, -1)

    low = jnp.einsum(
        "tbu,tyu->tby", hidden, adapter_down_weight, preferred_element_type=jnp.float32
    ).astype(jnp.bfloat16)
    where = jnp.concatenate([seq_index[None].astype(jnp.int32), lengths])
    rel = (offsets - seq_index * stretch_n).reshape(1, adapt_n * row_n)
    dquery, own_part, mid_part, far_part, swap_part = attention_grads(
        where,
        rel,
        response_base_queries,
        attention_output_gradient,
        low,
        adapter_up_weight,
        own,
        mid,
        far,
        swap,
    )
    far_back = moved(far_part, -3, -1)
    swap_back = moved(swap_part, 1, -1)
    mid_back = moved((mid_part + swap_back.astype(jnp.float32)).astype(jnp.bfloat16), -2, -2)
    prompt = own_part + far_back.astype(jnp.float32) + mid_back.astype(jnp.float32)
    prompt = prompt.astype(jnp.bfloat16).reshape(planes, stretch_n // planes, 2 * head_dim)
    prompt = lax.all_to_all(prompt, "adapter", 0, 0, tiled=True).astype(jnp.float32).sum(0)

    blocks = adapter_grads(dquery, low, adapter_up_weight, hidden, inner, outer)
    near = [[g * inner + i for i in range(inner)] for g in range(outer)]
    across = [[g * inner + i for g in range(outer)] for i in range(inner)]
    blocks = grouped(blocks, near).astype(jnp.float32).sum(0)
    up_copies = jnp.broadcast_to(blocks[outer:], blocks[:outer].shape)
    blocks = grouped(jnp.stack([blocks[:outer], up_copies], axis=1), across).sum(0)
    down = blocks[0].reshape(adapt_n, rank, -1)
    up_blocks = grouped(jnp.broadcast_to(blocks[1:], (inner,) + blocks.shape[1:]), near)
    up_gradient = up_blocks.reshape(inner, adapt_n, rank, -1).transpose(1, 2, 0, 3)
    return (
        down,
        up_gradient.reshape(adapt_n, rank, feature_n),
        prompt[:, :head_dim],
        prompt[:, head_dim:],
    )


def solution(mesh):
    return jax.shard_map(
        local,
        mesh=mesh,
        in_specs=(
            P("adapter", "seq", None),
            P("adapter", "seq", None),
            P("adapter", "seq", None),
            P("seq", None),
            P("seq", None),
            P("adapter", None, None),
            P("adapter", None, None),
            P("adapter"),
            P("adapter", "seq"),
        ),
        out_specs=(
            P("adapter", None, "seq"),
            P("adapter", None, None),
            P(("seq", "adapter"), None),
            P(("seq", "adapter"), None),
        ),
        check_vma=False,
    )
```

```python
import functools

import jax
import jax.numpy as jnp
from jax import lax
from jax.experimental import pallas as pl
from jax.experimental.pallas import tpu as pltpu
from jax.sharding import PartitionSpec as P

adapter_scale = 2.0
masked_score = -1.0e30
log2_e = 1.4426950408889634
both_axes = ("seq", "adapter")
row_n_seq = 8

NN = ((1,), (0,))
NT = ((1,), (1,))


def dot(a, b, dims):
    return lax.dot_general(a, b, (dims, ((), ())), preferred_element_type=jnp.float32)


def moved(value, by_even, by_odd):
    peers, planes = lax.axis_size("seq"), lax.axis_size("adapter")
    pairs = []
    for s in range(peers):
        t = s + (by_odd if s % 2 else by_even)
        if 0 <= t < peers:
            for a in range(planes):
                b = a if t // row_n_seq == s // row_n_seq else planes - 1 - a
                pairs.append((s * planes + a, t * planes + b))
    return lax.ppermute(value, both_axes, pairs)


def grouped(value, groups):
    return lax.all_to_all(value, "seq", 0, 0, axis_index_groups=groups, tiled=True)


def spans_of(stretch, count=4):
    return [slice(d * stretch, (d + 1) * stretch) for d in range(count)]


def fill_window(window, odd, own, mid, far, swap):
    spans = spans_of(own.shape[0])
    window[spans[0], :] = own[...]
    window[spans[2], :] = mid[...]

    @pl.when(odd)
    def _():
        window[spans[1], :] = far[...]
        window[spans[3], :] = swap[...]

    @pl.when(jnp.logical_not(odd))
    def _():
        window[spans[1], :] = swap[...]
        window[spans[3], :] = far[...]


def fill_plain(window, blocks):
    for span, block in zip(spans_of(blocks[0].shape[0]), blocks):
        window[span, :] = block[...]


def empty_window(acc, odd, factor, own, mid, far, swap):
    spans = spans_of(own.shape[0])

    def put(out, span):
        out[...] = (acc[span, :] * factor).astype(out.dtype)

    put(own, spans[0])
    put(mid, spans[2])

    @pl.when(odd)
    def _():
        put(far, spans[1])
        put(swap, spans[3])

    @pl.when(jnp.logical_not(odd))
    def _():
        put(far, spans[3])
        put(swap, spans[1])


def fold(x, op):
    return op(x.reshape(x.shape[0] // 8, 8, x.shape[1]), axis=0)


def chunks(stretch, chunk):
    for d in range(3):
        for c in range(0, stretch, chunk):
            yield d, c, slice(d * stretch + c, d * stretch + c + chunk)


def prob_kernel(
    where_ref, rel_ref, base_ref, grad_ref, low_ref, up_ref, own, mid, far, swap,
    raised_ref, scale_ref, query_ref, grad_use_ref, own_part, part_1, part_2, part_3,
    window, acc,
    *, stretch, chunk, rows, adapters, head_dim, heads,
):
    head = pl.program_id(0)
    shift = head_dim**-0.5 * log2_e
    wide = rows * adapters
    block = where_ref[0]
    odd = lax.rem(block, 2) == 1

    @pl.when(head == 0)
    def _():
        acc[...] = jnp.zeros_like(acc)
        fill_window(window, odd, own, mid, far, swap)

    line = block * rows + lax.broadcasted_iota(jnp.int32, (rows, head_dim), 0)
    for a in range(adapters):
        at = slice(a * rows, (a + 1) * rows)
        up = dot(low_ref[a], up_ref[a], NN)
        query_ref[at, :] = (base_ref[a].astype(jnp.float32) + adapter_scale * up).astype(
            jnp.bfloat16
        )
        live = line < where_ref[1 + a]
        grad_use_ref[at, :] = jnp.where(live, grad_ref[a].astype(jnp.float32), 0.0).astype(
            jnp.bfloat16
        )
    query = query_ref[...]
    grad = grad_use_ref[...]
    rel = rel_ref[...]
    place = lax.broadcasted_iota(jnp.int32, (chunk, wide), 0)
    bias3 = jnp.where(block >= 3, 0.0, masked_score)

    highs = [None] * 3
    for d, c, at in chunks(stretch, chunk):
        s = dot(window[at, :], query, NT)
        if d == 0:
            far_at = slice(3 * stretch + c, 3 * stretch + c + chunk)
            s = jnp.where(rel >= place + c, s, dot(window[far_at, :], query, NT) + bias3)
        raised_ref[0, at, :] = s
        top = fold(s, jnp.max)
        highs[d] = top if highs[d] is None else jnp.maximum(highs[d], top)
    peak = highs[0]
    for d in (1, 2):
        peak = jnp.maximum(peak, jnp.where(block >= d, highs[d], masked_score))
    peak = jnp.max(peak, axis=0, keepdims=True)
    total = jnp.zeros((8, wide), jnp.float32)
    levels = [peak] + [jnp.where(block >= d, peak, -masked_score) for d in (1, 2)]
    for d, c, at in chunks(stretch, chunk):
        e = jnp.exp2((raised_ref[0, at, :] - levels[d]) * shift)
        raised_ref[0, at, :] = e
        total = total + fold(e, jnp.sum)
    scale = 1.0 / jnp.sum(total, axis=0, keepdims=True)
    scale_ref[0] = scale
    for d, c, at in chunks(stretch, chunk):
        p = raised_ref[0, at, :] * scale
        if d == 0:
            early = rel >= place + c
            zero = jnp.zeros_like(p)
            far_at = slice(3 * stretch + c, 3 * stretch + c + chunk)
            late = jnp.where(early, zero, p).astype(jnp.bfloat16)
            acc[far_at, :] += dot(late, grad, NN)
            p = jnp.where(early, p, zero)
        acc[at, :] += dot(p.astype(jnp.bfloat16), grad, NN)

    @pl.when(head == heads - 1)
    def _():
        for span, out in zip(spans_of(stretch), (own_part, part_1, part_2, part_3)):
            out[...] = acc[span, :].astype(out.dtype)


def dscore_kernel(
    where_ref, rel_ref, raised_ref, scale_ref, query_ref, grad_use_ref,
    own, mid, far, swap, own_v, back_1, back_2, back_3,
    dquery_ref, own_part, mid_part, far_part, swap_part,
    window, window_v, key_t, dprob, dscore_low, acc,
    *, stretch, chunk, rows, adapters, head_dim, heads,
):
    head = pl.program_id(0)
    factor = head_dim**-0.5
    wide = rows * adapters
    odd = lax.rem(where_ref[0], 2) == 1

    @pl.when(head == 0)
    def _():
        acc[...] = jnp.zeros_like(acc)
        fill_window(window, odd, own, mid, far, swap)
        fill_plain(window_v, (own_v, back_1, back_2, back_3))
        for span in spans_of(stretch):
            key_t[:, span] = window[span, :].T

    query = query_ref[...]
    grad = grad_use_ref[...]
    rel = rel_ref[...]
    scale = scale_ref[0]
    place = lax.broadcasted_iota(jnp.int32, (chunk, wide), 0)
    delta = jnp.zeros((8, wide), jnp.float32)
    for d, c, at in chunks(stretch, chunk):
        dp = dot(window_v[at, :], grad, NT)
        if d == 0:
            far_at = slice(3 * stretch + c, 3 * stretch + c + chunk)
            dp = jnp.where(rel >= place + c, dp, dot(window_v[far_at, :], grad, NT))
        dprob[at, :] = dp
        delta = delta + fold(raised_ref[0, at, :] * dp, jnp.sum)
    delta = jnp.sum(delta, axis=0, keepdims=True) * scale
    for d, c, at in chunks(stretch, chunk):
        ds = (raised_ref[0, at, :] * scale) * (dprob[at, :] - delta)
        if d == 0:
            early = rel >= place + c
            zero = jnp.zeros_like(ds)
            far_at = slice(3 * stretch + c, 3 * stretch + c + chunk)
            late = jnp.where(early, zero, ds).astype(jnp.bfloat16)
            dscore_low[far_at, :] = late
            acc[far_at, :] += dot(late, query, NN)
            ds = jnp.where(early, ds, zero)
        low = ds.astype(jnp.bfloat16)
        dscore_low[at, :] = low
        acc[at, :] += dot(low, query, NN)
    dquery = (dot(key_t[...], dscore_low[...], NN).T * factor).astype(jnp.bfloat16)
    for a in range(adapters):
        dquery_ref[a] = dquery[a * rows : (a + 1) * rows]

    @pl.when(head == heads - 1)
    def _():
        empty_window(acc, odd, factor, own_part, mid_part, far_part, swap_part)


def sizes_of(base, own):
    adapters, rows, features = base.shape
    stretch, head_dim = own.shape
    return dict(
        stretch=stretch,
        chunk=256,
        rows=rows,
        adapters=adapters,
        head_dim=head_dim,
        heads=features // head_dim,
    )


def whole(*shape):
    return pl.BlockSpec(shape, lambda h, w: (0,) * len(shape))


def parts_of(stretch, head_dim, wide_n):
    return [
        jax.ShapeDtypeStruct((stretch, head_dim), jnp.float32 if d < wide_n else jnp.bfloat16)
        for d in range(4)
    ]


def prob_pass(where, rel, base, grad, low, up, own, mid, far, swap):
    sizes = sizes_of(base, own)
    adapters, rows, heads = sizes["adapters"], sizes["rows"], sizes["heads"]
    stretch, head_dim = own.shape
    rank, wide = low.shape[2], rows * adapters
    per_head = pl.BlockSpec((adapters, rows, head_dim), lambda h, w: (0, 0, h))
    flat = pl.BlockSpec((wide, head_dim), lambda h, w: (0, h))
    return pl.pallas_call(
        functools.partial(prob_kernel, **sizes),
        grid_spec=pltpu.PrefetchScalarGridSpec(
            num_scalar_prefetch=1,
            grid=(heads,),
            in_specs=[
                whole(1, wide),
                per_head,
                per_head,
                whole(adapters, rows, rank),
                pl.BlockSpec((adapters, rank, head_dim), lambda h, w: (0, 0, h)),
            ]
            + [whole(stretch, head_dim)] * 4,
            out_specs=[
                pl.BlockSpec((1, 3 * stretch, wide), lambda h, w: (h, 0, 0)),
                pl.BlockSpec((1, 1, wide), lambda h, w: (h, 0, 0)),
                flat,
                flat,
            ]
            + [whole(stretch, head_dim)] * 4,
            scratch_shapes=[
                pltpu.VMEM((4 * stretch, head_dim), jnp.bfloat16),
                pltpu.VMEM((4 * stretch, head_dim), jnp.float32),
            ],
        ),
        out_shape=[
            jax.ShapeDtypeStruct((heads, 3 * stretch, wide), jnp.float32),
            jax.ShapeDtypeStruct((heads, 1, wide), jnp.float32),
            jax.ShapeDtypeStruct((wide, heads * head_dim), jnp.bfloat16),
            jax.ShapeDtypeStruct((wide, heads * head_dim), jnp.bfloat16),
        ]
        + parts_of(stretch, head_dim, 1),
        compiler_params=pltpu.CompilerParams(
            dimension_semantics=("arbitrary",), vmem_limit_bytes=32 * 1024 * 1024
        ),
        name="prob_pass",
    )(where, rel, base, grad, low, up, own, mid, far, swap)


def dscore_pass(where, rel, base, raised, scale, query, grad_use, key_blocks, value_blocks):
    sizes = sizes_of(base, key_blocks[0])
    adapters, rows, heads = sizes["adapters"], sizes["rows"], sizes["heads"]
    stretch, head_dim = key_blocks[0].shape
    wide = rows * adapters
    flat = pl.BlockSpec((wide, head_dim), lambda h, w: (0, h))
    return pl.pallas_call(
        functools.partial(dscore_kernel, **sizes),
        grid_spec=pltpu.PrefetchScalarGridSpec(
            num_scalar_prefetch=1,
            grid=(heads,),
            in_specs=[
                whole(1, wide),
                pl.BlockSpec((1, 3 * stretch, wide), lambda h, w: (h, 0, 0)),
                pl.BlockSpec((1, 1, wide), lambda h, w: (h, 0, 0)),
                flat,
                flat,
            ]
            + [whole(stretch, head_dim)] * 8,
            out_specs=[pl.BlockSpec((adapters, rows, head_dim), lambda h, w: (0, 0, h))]
            + [whole(stretch, head_dim)] * 4,
            scratch_shapes=[
                pltpu.VMEM((4 * stretch, head_dim), jnp.bfloat16),
                pltpu.VMEM((4 * stretch, head_dim), jnp.bfloat16),
                pltpu.VMEM((head_dim, 4 * stretch), jnp.bfloat16),
                pltpu.VMEM((3 * stretch, wide), jnp.float32),
                pltpu.VMEM((4 * stretch, wide), jnp.bfloat16),
                pltpu.VMEM((4 * stretch, head_dim), jnp.float32),
            ],
        ),
        out_shape=[jax.ShapeDtypeStruct(base.shape, jnp.bfloat16)] + parts_of(stretch, head_dim, 2),
        compiler_params=pltpu.CompilerParams(
            dimension_semantics=("arbitrary",), vmem_limit_bytes=32 * 1024 * 1024
        ),
        name="dscore_pass",
    )(where, rel, raised, scale, query, grad_use, *key_blocks, *value_blocks)


def adapter_kernel(
    where_ref, dquery_ref, low_ref, up_ref, hidden_ref, keep_ref, send_ref, small,
    *, adapters, rank, lanes, chips,
):
    step = pl.program_id(0)
    outer = pl.num_programs(0)
    odd = lax.rem(where_ref[0], 2)

    def put(core, place, at, value):
        @pl.when(odd == core)
        def _():
            keep_ref[place, at, :] = value

        @pl.when(odd != core)
        def _():
            send_ref[place, at, :] = value.astype(send_ref.dtype)

    @pl.when(step == 0)
    def _():
        for a in range(adapters):
            at = slice(a * rank, (a + 1) * rank)
            small[at, :] = dot(up_ref[a], dquery_ref[a], NT).astype(jnp.bfloat16)
            low_t = low_ref[a].astype(jnp.float32).T.astype(jnp.bfloat16)
            piece = adapter_scale * dot(low_t, dquery_ref[a], NN)
            for i in range(2 * chips):
                put(i // chips, chips * outer + i % chips, at, piece[:, i * lanes : (i + 1) * lanes])

    for a in range(adapters):
        at = slice(a * rank, (a + 1) * rank)
        piece = adapter_scale * dot(small[at, :], hidden_ref[a], NN)
        for i in range(2 * chips):
            put(i % 2, (i // 2) * outer + step, at, piece[:, i * lanes : (i + 1) * lanes])


def adapter_grads(where, dquery, low, up, hidden, chips, outer):
    adapters, rows, features = dquery.shape
    rank = low.shape[2]
    width = hidden.shape[2]
    lanes = width // (2 * chips * outer)
    shape = ((outer + 1) * chips, adapters * rank, lanes)
    return pl.pallas_call(
        functools.partial(adapter_kernel, adapters=adapters, rank=rank, lanes=lanes, chips=chips),
        grid_spec=pltpu.PrefetchScalarGridSpec(
            num_scalar_prefetch=1,
            grid=(outer,),
            in_specs=[
                whole(adapters, rows, features),
                whole(adapters, rows, rank),
                whole(adapters, rank, features),
                pl.BlockSpec((adapters, rows, 2 * chips * lanes), lambda g, w: (0, 0, g)),
            ],
            out_specs=[whole(*shape), whole(*shape)],
            scratch_shapes=[pltpu.VMEM((adapters * rank, rows), jnp.bfloat16)],
        ),
        out_shape=[
            jax.ShapeDtypeStruct(shape, jnp.float32),
            jax.ShapeDtypeStruct(shape, jnp.bfloat16),
        ],
        compiler_params=pltpu.CompilerParams(
            dimension_semantics=("arbitrary",), vmem_limit_bytes=24 * 1024 * 1024
        ),
        name="adapter_grads",
    )(where, dquery, low, up, hidden)


def local(
    hidden,
    response_base_queries,
    attention_output_gradient,
    keys,
    values,
    adapter_down_weight,
    adapter_up_weight,
    lengths,
    offsets,
):
    adapt_n, row_n, feature_n = response_base_queries.shape
    rank = adapter_down_weight.shape[1]
    stretch_n, head_dim = keys.shape
    seq_index = lax.axis_index("seq")
    odd = seq_index % 2 == 1
    planes = lax.axis_size("adapter")
    chips = row_n_seq // 2
    outer = lax.axis_size("seq") // row_n_seq

    mid_k, far_k = moved(keys, 2, 2), moved(keys, 1, 3)
    value_blocks = [values] + [moved(values, d, d) for d in (1, 2, 3)]
    low = jnp.einsum(
        "tbu,tyu->tby", hidden, adapter_down_weight, preferred_element_type=jnp.float32
    ).astype(jnp.bfloat16)
    where = jnp.concatenate([seq_index[None].astype(jnp.int32), lengths])
    rel = (offsets - seq_index * stretch_n).reshape(1, adapt_n * row_n)
    mid_k, low, where, rel = lax.optimization_barrier((mid_k, low, where, rel))
    swap_k = moved(mid_k, 1, -1)
    key_blocks = (keys, mid_k, far_k, swap_k)
    raised, scale, query, grad_use, *value_parts = prob_pass(
        where,
        rel,
        response_base_queries,
        attention_output_gradient,
        low,
        adapter_up_weight,
        *key_blocks,
    )
    value_backs = [moved(part, -d, -d) for d, part in enumerate(value_parts) if d]
    dquery, own_dk, mid_dk, far_dk, swap_dk = dscore_pass(
        where,
        rel,
        response_base_queries,
        raised,
        scale,
        query,
        grad_use,
        key_blocks,
        value_blocks,
    )
    keep, send = adapter_grads(where, dquery, low, adapter_up_weight, hidden, chips, outer)
    far_back = moved(far_dk, -3, -1)
    swap_back = moved(swap_dk, 1, -1)
    swap_back, _ = lax.optimization_barrier((swap_back, send))
    mid_dk = (mid_dk + swap_back.astype(jnp.float32)).astype(jnp.bfloat16)

    n_down = chips * outer
    lanes = keep.shape[2]
    at_core = keep + moved(send, 1, -1).astype(jnp.float32)
    at_core = at_core.astype(jnp.bfloat16)
    up_copies = jnp.broadcast_to(at_core[None, n_down:], (chips, chips) + at_core.shape[1:])
    at_core = jnp.concatenate(
        [at_core[:n_down].reshape(chips, outer, adapt_n * rank, lanes), up_copies], axis=1
    )
    at_core, _ = lax.optimization_barrier((at_core, mid_dk))
    mid_back = moved(mid_dk, -2, -2)
    along_x = [[(g * chips + x) * 2 + c for x in range(chips)] for g in range(outer) for c in range(2)]
    at_chip = grouped(at_core, along_x).astype(jnp.float32).sum(0).astype(jnp.bfloat16)
    up_copies = jnp.broadcast_to(at_chip[None, outer:], (outer, chips) + at_chip.shape[1:])
    at_chip = jnp.concatenate([at_chip[:outer, None], up_copies], axis=1)
    mid_back, far_back, value_backs, _ = lax.optimization_barrier(
        (mid_back, far_back, value_backs, at_chip)
    )
    across = [[g * row_n_seq + i for g in range(outer)] for i in range(row_n_seq)]
    summed = grouped(at_chip, across).astype(jnp.float32).sum(0)

    key_total = own_dk + far_back.astype(jnp.float32) + mid_back.astype(jnp.float32)
    value_total = value_parts[0] + sum(back.astype(jnp.float32) for back in value_backs)
    prompt = jnp.stack([key_total, value_total]).astype(jnp.bfloat16)
    prompt = prompt.reshape(2, planes, stretch_n // planes, head_dim)
    prompt = lax.all_to_all(prompt, "adapter", 1, 1, tiled=True).astype(jnp.float32).sum(1)

    down = summed[0].reshape(adapt_n, rank, lanes)
    up_mine = summed[1:]
    up_other = moved(up_mine, 1, -1)
    up_blocks = jnp.concatenate(
        [jnp.where(odd, up_other, up_mine), jnp.where(odd, up_mine, up_other)], axis=0
    )
    up_blocks = up_blocks.reshape(2 * chips, adapt_n, rank, lanes).transpose(1, 2, 0, 3)
    return (down, up_blocks.reshape(adapt_n, rank, feature_n), prompt[0], prompt[1])


def solution(mesh):
    return jax.shard_map(
        local,
        mesh=mesh,
        in_specs=(
            P("adapter", "seq", None),
            P("adapter", "seq", None),
            P("adapter", "seq", None),
            P("seq", None),
            P("seq", None),
            P("adapter", None, None),
            P("adapter", None, None),
            P("adapter"),
            P("adapter", "seq"),
        ),
        out_specs=(
            P("adapter", None, "seq"),
            P("adapter", None, None),
            P(("seq", "adapter"), None),
            P(("seq", "adapter"), None),
        ),
        check_vma=False,
    )
```

```python
import functools

import jax
import jax.numpy as jnp
from jax import lax
from jax.experimental import pallas as pl
from jax.experimental.pallas import tpu as pltpu
from jax.sharding import PartitionSpec as P

adapter_scale = 2.0
masked_score = -1.0e30
log2_e = 1.4426950408889634
both_axes = ("seq", "adapter")
row_n_seq = 8

NN = ((1,), (0,))
NT = ((1,), (1,))


def dot(a, b, dims):
    return lax.dot_general(a, b, (dims, ((), ())), preferred_element_type=jnp.float32)


def moved(value, by_even, by_odd):
    peers, planes = lax.axis_size("seq"), lax.axis_size("adapter")
    pairs = []
    for s in range(peers):
        t = s + (by_odd if s % 2 else by_even)
        if 0 <= t < peers:
            for a in range(planes):
                b = a if t // row_n_seq == s // row_n_seq else planes - 1 - a
                pairs.append((s * planes + a, t * planes + b))
    return lax.ppermute(value, both_axes, pairs)


def grouped(value, groups):
    return lax.all_to_all(value, "seq", 0, 0, axis_index_groups=groups, tiled=True)


def attention_kernel(
    where_ref, rel_ref, base_ref, grad_ref, low_ref, up_ref, kv_own, kv_mid, kv_far, kv_swap,
    dquery_ref, own_ref, mid_ref, far_ref, swap_ref,
    window, key_t, score, dprob, dscore_low, acc,
    *, stretch, chunk, rows, adapters, head_dim, heads,
):
    head = pl.program_id(0)
    factor = head_dim**-0.5
    shift = factor * log2_e
    parts = stretch // chunk
    wide = rows * adapters
    block = where_ref[0]
    odd = lax.rem(block, 2) == 1
    spans = [slice(d * stretch, (d + 1) * stretch) for d in range(4)]

    @pl.when(head == 0)
    def _():
        acc[...] = jnp.zeros_like(acc)
        window[spans[0], :] = kv_own[...]
        window[spans[2], :] = kv_mid[...]

        @pl.when(odd)
        def _():
            window[spans[1], :] = kv_far[...]
            window[spans[3], :] = kv_swap[...]

        @pl.when(jnp.logical_not(odd))
        def _():
            window[spans[1], :] = kv_swap[...]
            window[spans[3], :] = kv_far[...]

        for span in spans:
            key_t[:, span] = window[span, :head_dim].T

    query_list = []
    grad_list = []
    line = block * rows + lax.broadcasted_iota(jnp.int32, (rows, head_dim), 0)
    for a in range(adapters):
        raised = dot(low_ref[a], up_ref[a], NN)
        query_list.append(
            (base_ref[a].astype(jnp.float32) + adapter_scale * raised).astype(jnp.bfloat16)
        )
        live = line < where_ref[1 + a]
        grad_list.append(
            jnp.where(live, grad_ref[a].astype(jnp.float32), 0.0).astype(jnp.bfloat16)
        )
    query = jnp.concatenate(query_list, axis=0)
    grad = jnp.concatenate(grad_list, axis=0)
    rel = rel_ref[...]
    place = lax.broadcasted_iota(jnp.int32, (chunk, wide), 0)
    bias3 = jnp.where(block >= 3, 0.0, masked_score)

    def fold(x, op):
        return op(x.reshape(x.shape[0] // 8, 8, x.shape[1]), axis=0)

    peak = None
    for d in range(3):
        high = None
        for c in range(parts):
            at = slice(d * stretch + c * chunk, d * stretch + (c + 1) * chunk)
            s = dot(window[at, :head_dim], query, NT)
            dp = dot(window[at, head_dim:], grad, NT)
            if d == 0:
                early = rel >= place + c * chunk
                far = slice(3 * stretch + c * chunk, 3 * stretch + (c + 1) * chunk)
                s = jnp.where(early, s, dot(window[far, :head_dim], query, NT) + bias3)
                dp = jnp.where(early, dp, dot(window[far, head_dim:], grad, NT))
            score[at, :] = s
            dprob[at, :] = dp
            top = fold(s, jnp.max)
            high = top if high is None else jnp.maximum(high, top)
        if d:
            high = jnp.where(block >= d, high, masked_score)
        peak = high if peak is None else jnp.maximum(peak, high)
    peak = jnp.max(peak, axis=0, keepdims=True)
    total = jnp.zeros((8, wide), jnp.float32)
    delta = jnp.zeros((8, wide), jnp.float32)
    for d in range(3):
        level = peak if d == 0 else jnp.where(block >= d, peak, -masked_score)
        for c in range(parts):
            at = slice(d * stretch + c * chunk, d * stretch + (c + 1) * chunk)
            e = jnp.exp2((score[at, :] - level) * shift)
            score[at, :] = e
            total = total + fold(e, jnp.sum)
            delta = delta + fold(e * dprob[at, :], jnp.sum)
    scale = 1.0 / jnp.sum(total, axis=0, keepdims=True)
    delta = jnp.sum(delta, axis=0, keepdims=True) * scale
    zero = jnp.zeros((chunk, wide), jnp.float32)
    for d in range(3):
        for c in range(parts):
            at = slice(d * stretch + c * chunk, d * stretch + (c + 1) * chunk)
            p = score[at, :] * scale
            ds = p * (dprob[at, :] - delta)
            if d == 0:
                early = rel >= place + c * chunk
                pieces = (
                    (0, jnp.where(early, p, zero), jnp.where(early, ds, zero)),
                    (3, jnp.where(early, zero, p), jnp.where(early, zero, ds)),
                )
            else:
                pieces = ((d, p, ds),)
            for e, p_e, ds_e in pieces:
                to = slice(e * stretch + c * chunk, e * stretch + (c + 1) * chunk)
                p_e = p_e.astype(jnp.bfloat16)
                ds_e = ds_e.astype(jnp.bfloat16)
                dscore_low[to, :] = ds_e
                acc[to, :head_dim] += dot(ds_e, query, NN)
                acc[to, head_dim:] += dot(p_e, grad, NN)
    dquery = (dot(key_t[...], dscore_low[...], NN).T * factor).astype(jnp.bfloat16)
    for a in range(adapters):
        dquery_ref[a] = dquery[a * rows : (a + 1) * rows]

    @pl.when(head == heads - 1)
    def _():
        def put(out, span):
            out[:, :head_dim] = (acc[span, :head_dim] * factor).astype(out.dtype)
            out[:, head_dim:] = acc[span, head_dim:].astype(out.dtype)

        put(own_ref, spans[0])
        put(mid_ref, spans[2])

        @pl.when(odd)
        def _():
            put(far_ref, spans[1])
            put(swap_ref, spans[3])

        @pl.when(jnp.logical_not(odd))
        def _():
            put(far_ref, spans[3])
            put(swap_ref, spans[1])


def attention_grads(where, rel, base, grad, low, up, own, mid, far, swap):
    adapters, rows, features = base.shape
    stretch, both = own.shape
    head_dim = both // 2
    heads = features // head_dim
    rank = low.shape[2]
    wide = rows * adapters
    body = functools.partial(
        attention_kernel,
        stretch=stretch,
        chunk=256,
        rows=rows,
        adapters=adapters,
        head_dim=head_dim,
        heads=heads,
    )
    per_head = pl.BlockSpec((adapters, rows, head_dim), lambda h, w: (0, 0, h))

    def whole(*shape):
        return pl.BlockSpec(shape, lambda h, w: (0,) * len(shape))

    return pl.pallas_call(
        body,
        grid_spec=pltpu.PrefetchScalarGridSpec(
            num_scalar_prefetch=1,
            grid=(heads,),
            in_specs=[
                whole(1, wide),
                per_head,
                per_head,
                whole(adapters, rows, rank),
                pl.BlockSpec((adapters, rank, head_dim), lambda h, w: (0, 0, h)),
            ]
            + [whole(stretch, both)] * 4,
            out_specs=[per_head] + [whole(stretch, both)] * 4,
            scratch_shapes=[
                pltpu.VMEM((4 * stretch, both), jnp.bfloat16),
                pltpu.VMEM((head_dim, 4 * stretch), jnp.bfloat16),
                pltpu.VMEM((3 * stretch, wide), jnp.float32),
                pltpu.VMEM((3 * stretch, wide), jnp.float32),
                pltpu.VMEM((4 * stretch, wide), jnp.bfloat16),
                pltpu.VMEM((4 * stretch, both), jnp.float32),
            ],
        ),
        out_shape=[
            jax.ShapeDtypeStruct(base.shape, jnp.bfloat16),
            jax.ShapeDtypeStruct((stretch, both), jnp.float32),
            jax.ShapeDtypeStruct((stretch, both), jnp.float32),
            jax.ShapeDtypeStruct((stretch, both), jnp.bfloat16),
            jax.ShapeDtypeStruct((stretch, both), jnp.bfloat16),
        ],
        compiler_params=pltpu.CompilerParams(
            dimension_semantics=("arbitrary",), vmem_limit_bytes=28 * 1024 * 1024
        ),
        name="attention_grads",
    )(where, rel, base, grad, low, up, own, mid, far, swap)


def whole(*shape):
    return pl.BlockSpec(shape, lambda h, w: (0,) * len(shape))


def adapter_kernel(
    where_ref, dquery_ref, low_ref, up_ref, hidden_ref, keep_ref, send_ref, small,
    *, adapters, rank, lanes, chips,
):
    step = pl.program_id(0)
    outer = pl.num_programs(0)
    odd = lax.rem(where_ref[0], 2)

    def put(core, place, at, value):
        @pl.when(odd == core)
        def _():
            keep_ref[place, at, :] = value

        @pl.when(odd != core)
        def _():
            send_ref[place, at, :] = value.astype(send_ref.dtype)

    @pl.when(step == 0)
    def _():
        for a in range(adapters):
            at = slice(a * rank, (a + 1) * rank)
            small[at, :] = dot(up_ref[a], dquery_ref[a], NT).astype(jnp.bfloat16)
            low_t = low_ref[a].astype(jnp.float32).T.astype(jnp.bfloat16)
            piece = adapter_scale * dot(low_t, dquery_ref[a], NN)
            for i in range(2 * chips):
                put(i // chips, chips * outer + i % chips, at, piece[:, i * lanes : (i + 1) * lanes])

    for a in range(adapters):
        at = slice(a * rank, (a + 1) * rank)
        piece = adapter_scale * dot(small[at, :], hidden_ref[a], NN)
        for i in range(2 * chips):
            put(i % 2, (i // 2) * outer + step, at, piece[:, i * lanes : (i + 1) * lanes])


def adapter_grads(where, dquery, low, up, hidden, chips, outer):
    adapters, rows, features = dquery.shape
    rank = low.shape[2]
    width = hidden.shape[2]
    lanes = width // (2 * chips * outer)
    shape = ((outer + 1) * chips, adapters * rank, lanes)
    return pl.pallas_call(
        functools.partial(adapter_kernel, adapters=adapters, rank=rank, lanes=lanes, chips=chips),
        grid_spec=pltpu.PrefetchScalarGridSpec(
            num_scalar_prefetch=1,
            grid=(outer,),
            in_specs=[
                whole(adapters, rows, features),
                whole(adapters, rows, rank),
                whole(adapters, rank, features),
                pl.BlockSpec((adapters, rows, 2 * chips * lanes), lambda g, w: (0, 0, g)),
            ],
            out_specs=[whole(*shape), whole(*shape)],
            scratch_shapes=[pltpu.VMEM((adapters * rank, rows), jnp.bfloat16)],
        ),
        out_shape=[
            jax.ShapeDtypeStruct(shape, jnp.float32),
            jax.ShapeDtypeStruct(shape, jnp.bfloat16),
        ],
        compiler_params=pltpu.CompilerParams(
            dimension_semantics=("arbitrary",), vmem_limit_bytes=24 * 1024 * 1024
        ),
        name="adapter_grads",
    )(where, dquery, low, up, hidden)


def local(
    hidden,
    response_base_queries,
    attention_output_gradient,
    keys,
    values,
    adapter_down_weight,
    adapter_up_weight,
    lengths,
    offsets,
):
    adapt_n, row_n, feature_n = response_base_queries.shape
    rank = adapter_down_weight.shape[1]
    stretch_n, head_dim = keys.shape
    seq_index = lax.axis_index("seq")
    odd = seq_index % 2 == 1
    planes = lax.axis_size("adapter")
    chips = row_n_seq // 2
    outer = lax.axis_size("seq") // row_n_seq

    own = jnp.concatenate([keys, values], axis=1)
    far = moved(own, 1, 3)
    mid = moved(own, 2, 2)
    low = jnp.einsum(
        "tbu,tyu->tby", hidden, adapter_down_weight, preferred_element_type=jnp.float32
    ).astype(jnp.bfloat16)
    where = jnp.concatenate([seq_index[None].astype(jnp.int32), lengths])
    rel = (offsets - seq_index * stretch_n).reshape(1, adapt_n * row_n)
    mid, low, where, rel = lax.optimization_barrier((mid, low, where, rel))
    swap = moved(mid, 1, -1)
    dquery, own_part, mid_part, far_part, swap_part = attention_grads(
        where,
        rel,
        response_base_queries,
        attention_output_gradient,
        low,
        adapter_up_weight,
        own,
        mid,
        far,
        swap,
    )
    far_back = moved(far_part, -3, -1)
    swap_back = moved(swap_part, 1, -1)
    keep, send = adapter_grads(where, dquery, low, adapter_up_weight, hidden, chips, outer)
    swap_back, keep, send = lax.optimization_barrier((swap_back, keep, send))
    mid_part = (mid_part + swap_back.astype(jnp.float32)).astype(jnp.bfloat16)
    mid_back = moved(mid_part, -2, -2)

    n_down = chips * outer
    lanes = keep.shape[2]
    at_core = keep + moved(send, 1, -1).astype(jnp.float32)
    at_core = at_core.astype(jnp.bfloat16)
    up_copies = jnp.broadcast_to(at_core[None, n_down:], (chips, chips) + at_core.shape[1:])
    at_core = jnp.concatenate(
        [at_core[:n_down].reshape(chips, outer, adapt_n * rank, lanes), up_copies], axis=1
    )
    along_x = [[(g * chips + x) * 2 + c for x in range(chips)] for g in range(outer) for c in range(2)]
    at_chip = grouped(at_core, along_x)
    at_chip, far_back = lax.optimization_barrier((at_chip, far_back))
    at_chip = at_chip.astype(jnp.float32).sum(0).astype(jnp.bfloat16)
    up_copies = jnp.broadcast_to(at_chip[None, outer:], (outer, chips) + at_chip.shape[1:])
    at_chip = jnp.concatenate([at_chip[:outer, None], up_copies], axis=1)
    across = [[g * row_n_seq + i for g in range(outer)] for i in range(row_n_seq)]
    summed = grouped(at_chip, across)
    prompt = own_part + far_back.astype(jnp.float32) + mid_back.astype(jnp.float32)
    prompt = prompt.reshape(planes, stretch_n // planes, 2 * head_dim)
    plane = lax.axis_index("adapter")
    total = lax.dynamic_index_in_dim(prompt, plane, 0, False)
    shares = []
    for other in range(1, planes):
        share = lax.dynamic_index_in_dim(prompt, plane ^ other, 0, False).astype(jnp.bfloat16)
        shares.append(lax.ppermute(share, "adapter", [(a, a ^ other) for a in range(planes)]))
    summed, shares = lax.optimization_barrier((summed, shares))
    prompt = total + sum(share.astype(jnp.float32) for share in shares)
    summed = summed.astype(jnp.float32).sum(0)

    down = summed[0].reshape(adapt_n, rank, lanes)
    up_mine = summed[1:]
    up_other = moved(up_mine, 1, -1)
    up_blocks = jnp.concatenate(
        [jnp.where(odd, up_other, up_mine), jnp.where(odd, up_mine, up_other)], axis=0
    )
    up_blocks = up_blocks.reshape(2 * chips, adapt_n, rank, lanes).transpose(1, 2, 0, 3)
    return (
        down,
        up_blocks.reshape(adapt_n, rank, feature_n),
        prompt[:, :head_dim],
        prompt[:, head_dim:],
    )


def solution(mesh):
    return jax.shard_map(
        local,
        mesh=mesh,
        in_specs=(
            P("adapter", "seq", None),
            P("adapter", "seq", None),
            P("adapter", "seq", None),
            P("seq", None),
            P("seq", None),
            P("adapter", None, None),
            P("adapter", None, None),
            P("adapter"),
            P("adapter", "seq"),
        ),
        out_specs=(
            P("adapter", None, "seq"),
            P("adapter", None, None),
            P(("seq", "adapter"), None),
            P(("seq", "adapter"), None),
        ),
        check_vma=False,
    )
```

```python
import functools

import jax
import jax.numpy as jnp
from jax import lax
from jax.experimental import pallas as pl
from jax.experimental.pallas import tpu as pltpu
from jax.sharding import PartitionSpec as P

adapter_scale = 2.0
masked_score = -1.0e30
log2_e = 1.4426950408889634
both_axes = ("seq", "adapter")
row_n_seq = 8

NN = ((1,), (0,))
NT = ((1,), (1,))


def dot(a, b, dims):
    return lax.dot_general(a, b, (dims, ((), ())), preferred_element_type=jnp.float32)


def moved(value, by_even, by_odd):
    peers, planes = lax.axis_size("seq"), lax.axis_size("adapter")
    pairs = []
    for s in range(peers):
        t = s + (by_odd if s % 2 else by_even)
        if 0 <= t < peers:
            for a in range(planes):
                b = a if t // row_n_seq == s // row_n_seq else planes - 1 - a
                pairs.append((s * planes + a, t * planes + b))
    return lax.ppermute(value, both_axes, pairs)


def grouped(value, groups):
    return lax.all_to_all(value, "seq", 0, 0, axis_index_groups=groups, tiled=True)


def fold(x, op):
    return op(x.reshape(x.shape[0] // 8, 8, x.shape[1]), axis=0)


def chunks(stretch, chunk):
    for d in range(3):
        for c in range(0, stretch, chunk):
            yield d, slice(c, c + chunk), slice(d * stretch + c, d * stretch + c + chunk)


def attention_kernel(
    where_ref, rel_ref, base_ref, grad_ref, low_ref, up_ref, up_whole_ref, own_in, mid_in, far_in, swap_in, hidden_in,
    own_ref, mid_ref, far_ref, swap_ref, keep_ref, send_ref,
    window_k, window_v, key_t, score, dprob, dscore_low, acc_k, acc_v, hidden, dquery, pieces, block_sems, hidden_sem,
    *, stretch, chunk, rows, adapters, head_dim, heads, per_step, rank, chips, outer,
):
    step = pl.program_id(0)
    factor = head_dim**-0.5
    shift = factor * log2_e
    wide = rows * adapters
    block = where_ref[0]
    odd = lax.rem(block, 2)
    far_slot = 3 - 2 * odd
    swap_slot = 1 + 2 * odd

    def fills():
        sources = ((0, own_in), (2, mid_in), (far_slot, far_in), (swap_slot, swap_in))
        for i, (slot, source) in enumerate(sources):
            yield pltpu.make_async_copy(source.at[0], window_k.at[slot], block_sems.at[2 * i])
            yield pltpu.make_async_copy(source.at[1], window_v.at[slot], block_sems.at[2 * i + 1])

    hidden_copy = pltpu.make_async_copy(hidden_in, hidden, hidden_sem)

    @pl.when(step == 0)
    def _():
        for copy in fills():
            copy.start()
        hidden_copy.start()
        acc_k[...] = jnp.zeros_like(acc_k)
        acc_v[...] = jnp.zeros_like(acc_v)
        for copy in fills():
            copy.wait()
        for d in range(4):
            key_t[:, d * stretch : (d + 1) * stretch] = window_k[d].T

    rel = rel_ref[...]
    place = lax.broadcasted_iota(jnp.int32, (chunk, wide), 0)
    line = block * rows + lax.broadcasted_iota(jnp.int32, (rows, head_dim), 0)
    bias3 = jnp.where(block >= 3, 0.0, masked_score)

    def scores_of(j):
        cols = slice(j * head_dim, (j + 1) * head_dim)
        query_list = []
        grad_list = []
        for a in range(adapters):
            raised = dot(low_ref[a], up_ref[a, :, cols], NN)
            query_list.append(
                (base_ref[a, :, cols].astype(jnp.float32) + adapter_scale * raised).astype(jnp.bfloat16)
            )
            live = line < where_ref[1 + a]
            grad_list.append(
                jnp.where(live, grad_ref[a, :, cols].astype(jnp.float32), 0.0).astype(jnp.bfloat16)
            )
        query = jnp.concatenate(query_list, axis=0)
        grad = jnp.concatenate(grad_list, axis=0)
        highs = [None] * 3
        for d, part, at in chunks(stretch, chunk):
            s = dot(window_k[d, part, :], query, NT)
            dp = dot(window_v[d, part, :], grad, NT)
            if d == 0:
                early = rel >= place + part.start
                s = jnp.where(early, s, dot(window_k[3, part, :], query, NT) + bias3)
                dp = jnp.where(early, dp, dot(window_v[3, part, :], grad, NT))
            score[j, at, :] = s
            dprob[j, at, :] = dp
            top = fold(s, jnp.max)
            highs[d] = top if highs[d] is None else jnp.maximum(highs[d], top)
        peak = highs[0]
        for d in (1, 2):
            peak = jnp.maximum(peak, jnp.where(block >= d, highs[d], masked_score))
        return query, grad, jnp.max(peak, axis=0, keepdims=True)

    def sums_of(j, query, grad, peak):
        levels = [peak] + [jnp.where(block >= d, peak, -masked_score) for d in (1, 2)]
        total = jnp.zeros((8, wide), jnp.float32)
        delta = jnp.zeros((8, wide), jnp.float32)
        for d, part, at in chunks(stretch, chunk):
            e = jnp.exp2((score[j, at, :] - levels[d]) * shift)
            score[j, at, :] = e
            total = total + fold(e, jnp.sum)
            delta = delta + fold(e * dprob[j, at, :], jnp.sum)
        scale = 1.0 / jnp.sum(total, axis=0, keepdims=True)
        return query, grad, scale, jnp.sum(delta, axis=0, keepdims=True) * scale

    def grads_of(j, query, grad, scale, delta):
        for d, part, at in chunks(stretch, chunk):
            p = score[j, at, :] * scale
            ds = p * (dprob[j, at, :] - delta)
            if d == 0:
                early = rel >= place + part.start
                zero = jnp.zeros_like(p)
                split = (
                    (0, jnp.where(early, p, zero), jnp.where(early, ds, zero)),
                    (3, jnp.where(early, zero, p), jnp.where(early, zero, ds)),
                )
            else:
                split = ((d, p, ds),)
            for e, p_e, ds_e in split:
                ds_e = ds_e.astype(jnp.bfloat16)
                dscore_low[j, e * stretch + part.start : e * stretch + part.stop, :] = ds_e
                acc_k[e, part, :] += dot(ds_e, query, NN)
                acc_v[e, part, :] += dot(p_e.astype(jnp.bfloat16), grad, NN)
        part = (dot(key_t[...], dscore_low[j], NN).T * factor).astype(jnp.bfloat16)
        for a in range(adapters):
            dquery[step * per_step + j, a] = part[a * rows : (a + 1) * rows]

    states = [scores_of(j) for j in range(per_step)]
    for j in range(per_step):
        grads_of(j, *sums_of(j, *states[j]))

    @pl.when(step == heads // per_step - 1)
    def _():
        def put(out, slot):
            out[0] = (acc_k[slot] * factor).astype(out.dtype)
            out[1] = acc_v[slot].astype(out.dtype)

        put(own_ref, 0)
        put(mid_ref, 2)
        put(far_ref, far_slot)
        put(swap_ref, swap_slot)
        hidden_copy.wait()
        span = 2 * chips * head_dim
        for a in range(adapters):
            at = slice(a * rank, (a + 1) * rank)
            low_t = low_ref[a].astype(jnp.float32).T.astype(jnp.bfloat16)
            small = jnp.zeros((rank, rows), jnp.float32)
            for h in range(heads):
                mine = dquery[h, a]
                small += dot(up_whole_ref[a, :, h * head_dim : (h + 1) * head_dim], mine, NT)
                pieces[h // chips, chips * outer + h % chips, at, :] = adapter_scale * dot(
                    low_t, mine, NN
                )
            small_low = small.astype(jnp.bfloat16)
            for g in range(outer):
                piece = dot(small_low, hidden[a, :, g * span : (g + 1) * span], NN) * adapter_scale
                for i in range(2 * chips):
                    pieces[i % 2, (i // 2) * outer + g, at, :] = piece[
                        :, i * head_dim : (i + 1) * head_dim
                    ]
        keep_ref[...] = pieces[odd]
        send_ref[...] = pieces[1 - odd].astype(send_ref.dtype)


def whole(*shape):
    return pl.BlockSpec(shape, lambda h, w: (0,) * len(shape))


def attention_grads(where, rel, base, grad, low, up, own, mid, far, swap, hidden, chips, outer):
    adapters, rows, features = base.shape
    _, stretch, head_dim = own.shape
    heads = features // head_dim
    rank, wide, width = low.shape[2], rows * adapters, hidden.shape[2]
    per_step = 2
    assert heads == 2 * chips and width == 2 * chips * outer * head_dim
    body = functools.partial(
        attention_kernel,
        stretch=stretch,
        chunk=384,
        rows=rows,
        adapters=adapters,
        head_dim=head_dim,
        heads=heads,
        per_step=per_step,
        rank=rank,
        chips=chips,
        outer=outer,
    )
    per_head = pl.BlockSpec((adapters, rows, per_step * head_dim), lambda h, w: (0, 0, h))
    anywhere = pl.BlockSpec(memory_space=pltpu.HBM)
    blocks = (chips * outer + chips, adapters * rank, head_dim)
    pair = (2, stretch, head_dim)
    return pl.pallas_call(
        body,
        grid_spec=pltpu.PrefetchScalarGridSpec(
            num_scalar_prefetch=1,
            grid=(heads // per_step,),
            in_specs=[
                whole(1, wide),
                per_head,
                per_head,
                whole(adapters, rows, rank),
                pl.BlockSpec((adapters, rank, per_step * head_dim), lambda h, w: (0, 0, h)),
                whole(adapters, rank, features),
            ]
            + [anywhere] * 5,
            out_specs=[whole(*pair)] * 4 + [whole(*blocks)] * 2,
            scratch_shapes=[
                pltpu.VMEM((4, stretch, head_dim), jnp.bfloat16),
                pltpu.VMEM((4, stretch, head_dim), jnp.bfloat16),
                pltpu.VMEM((head_dim, 4 * stretch), jnp.bfloat16),
                pltpu.VMEM((per_step, 3 * stretch, wide), jnp.float32),
                pltpu.VMEM((per_step, 3 * stretch, wide), jnp.float32),
                pltpu.VMEM((per_step, 4 * stretch, wide), jnp.bfloat16),
                pltpu.VMEM((4, stretch, head_dim), jnp.float32),
                pltpu.VMEM((4, stretch, head_dim), jnp.float32),
                pltpu.VMEM((adapters, rows, width), jnp.bfloat16),
                pltpu.VMEM((heads, adapters, rows, head_dim), jnp.bfloat16),
                pltpu.VMEM((2,) + blocks, jnp.float32),
                pltpu.SemaphoreType.DMA((8,)),
                pltpu.SemaphoreType.DMA,
            ],
        ),
        out_shape=[
            jax.ShapeDtypeStruct(pair, kind)
            for kind in (jnp.float32, jnp.float32, jnp.bfloat16, jnp.bfloat16)
        ]
        + [jax.ShapeDtypeStruct(blocks, jnp.float32), jax.ShapeDtypeStruct(blocks, jnp.bfloat16)],
        compiler_params=pltpu.CompilerParams(
            dimension_semantics=("arbitrary",), vmem_limit_bytes=58 * 1024 * 1024
        ),
        name="attention_grads",
    )(where, rel, base, grad, low, up, up, own, mid, far, swap, hidden)


def local(
    hidden,
    response_base_queries,
    attention_output_gradient,
    keys,
    values,
    adapter_down_weight,
    adapter_up_weight,
    lengths,
    offsets,
):
    adapt_n, row_n, feature_n = response_base_queries.shape
    rank = adapter_down_weight.shape[1]
    stretch_n, head_dim = keys.shape
    seq_index = lax.axis_index("seq")
    odd = seq_index % 2 == 1
    planes = lax.axis_size("adapter")
    chips = row_n_seq // 2
    outer = lax.axis_size("seq") // row_n_seq

    own = jnp.stack([keys, values])
    far = moved(own, 1, 3)
    mid = moved(own, 2, 2)
    low = jnp.einsum(
        "tbu,tyu->tby", hidden, adapter_down_weight, preferred_element_type=jnp.float32
    ).astype(jnp.bfloat16)
    where = jnp.concatenate([seq_index[None].astype(jnp.int32), lengths])
    rel = (offsets - seq_index * stretch_n).reshape(1, adapt_n * row_n)
    mid, low, where, rel = lax.optimization_barrier((mid, low, where, rel))
    swap = moved(mid, 1, -1)
    own_part, mid_part, far_part, swap_part, keep, send = attention_grads(
        where,
        rel,
        response_base_queries,
        attention_output_gradient,
        low,
        adapter_up_weight,
        own,
        mid,
        far,
        swap,
        hidden,
        chips,
        outer,
    )
    far_back = moved(far_part, -3, -1)
    swap_back = moved(swap_part, 1, -1)
    mid_part = (mid_part + swap_back.astype(jnp.float32)).astype(jnp.bfloat16)
    mid_back = moved(mid_part, -2, -2)

    n_down = chips * outer
    lanes = keep.shape[2]
    at_core = keep + moved(send, 1, -1).astype(jnp.float32)
    at_core = at_core.astype(jnp.bfloat16)
    up_copies = jnp.broadcast_to(at_core[None, n_down:], (chips, chips) + at_core.shape[1:])
    at_core = jnp.concatenate(
        [at_core[:n_down].reshape(chips, outer, adapt_n * rank, lanes), up_copies], axis=1
    )
    along_x = [[(g * chips + x) * 2 + c for x in range(chips)] for g in range(outer) for c in range(2)]
    at_chip = grouped(at_core, along_x)
    at_chip, far_back = lax.optimization_barrier((at_chip, far_back))
    at_chip = at_chip.astype(jnp.float32).sum(0).astype(jnp.bfloat16)
    up_copies = jnp.broadcast_to(at_chip[None, outer:], (outer, chips) + at_chip.shape[1:])
    at_chip = jnp.concatenate([at_chip[:outer, None], up_copies], axis=1)
    across = [[g * row_n_seq + i for g in range(outer)] for i in range(row_n_seq)]
    summed = grouped(at_chip, across)
    prompt = own_part + far_back.astype(jnp.float32) + mid_back.astype(jnp.float32)
    prompt = prompt.reshape(2, planes, stretch_n // planes, head_dim)
    plane = lax.axis_index("adapter")
    total = lax.dynamic_index_in_dim(prompt, plane, 1, False)
    shares = []
    for other in range(1, planes):
        share = lax.dynamic_index_in_dim(prompt, plane ^ other, 1, False).astype(jnp.bfloat16)
        shares.append(lax.ppermute(share, "adapter", [(a, a ^ other) for a in range(planes)]))
    summed, shares = lax.optimization_barrier((summed, shares))
    prompt = total + sum(share.astype(jnp.float32) for share in shares)
    summed = summed.astype(jnp.float32).sum(0)

    down = summed[0].reshape(adapt_n, rank, lanes)
    up_mine = summed[1:]
    up_other = moved(up_mine, 1, -1)
    up_blocks = jnp.concatenate(
        [jnp.where(odd, up_other, up_mine), jnp.where(odd, up_mine, up_other)], axis=0
    )
    up_blocks = up_blocks.reshape(2 * chips, adapt_n, rank, lanes).transpose(1, 2, 0, 3)
    return (
        down,
        up_blocks.reshape(adapt_n, rank, feature_n),
        prompt[0],
        prompt[1],
    )


def solution(mesh):
    return jax.shard_map(
        local,
        mesh=mesh,
        in_specs=(
            P("adapter", "seq", None),
            P("adapter", "seq", None),
            P("adapter", "seq", None),
            P("seq", None),
            P("seq", None),
            P("adapter", None, None),
            P("adapter", None, None),
            P("adapter"),
            P("adapter", "seq"),
        ),
        out_specs=(
            P("adapter", None, "seq"),
            P("adapter", None, None),
            P(("seq", "adapter"), None),
            P(("seq", "adapter"), None),
        ),
        check_vma=False,
    )
```

```python
import functools

import jax
import jax.numpy as jnp
from jax import lax
from jax.experimental import pallas as pl
from jax.experimental.pallas import tpu as pltpu
from jax.sharding import PartitionSpec as P

adapter_scale = 2.0
masked_score = -1.0e30
log2_e = 1.4426950408889634
both_axes = ("seq", "adapter")
row_n_seq = 8

NN = ((1,), (0,))
NT = ((1,), (1,))


def dot(a, b, dims):
    return lax.dot_general(a, b, (dims, ((), ())), preferred_element_type=jnp.float32)


def moved(value, by_even, by_odd):
    peers, planes = lax.axis_size("seq"), lax.axis_size("adapter")
    pairs = []
    for s in range(peers):
        t = s + (by_odd if s % 2 else by_even)
        if 0 <= t < peers:
            for a in range(planes):
                b = a if t // row_n_seq == s // row_n_seq else planes - 1 - a
                pairs.append((s * planes + a, t * planes + b))
    return lax.ppermute(value, both_axes, pairs)


def moved_two_ahead(value):
    peers, planes = lax.axis_size("seq"), lax.axis_size("adapter")
    last = row_n_seq - 2
    onward, over = [], []
    for s in range(peers):
        t = s - last if s % row_n_seq >= last else s + 2
        for a in range(planes):
            onward.append((s * planes + a, t * planes + a))
            if s % row_n_seq < 2 and s + row_n_seq < peers:
                over.append((s * planes + a, (s + row_n_seq) * planes + planes - 1 - a))
    value = lax.ppermute(value, both_axes, onward)
    relayed = lax.ppermute(value, both_axes, over)
    return jnp.where(lax.axis_index("seq") % row_n_seq < 2, relayed, value)


def round_x_back(value):
    peers, planes = lax.axis_size("seq"), lax.axis_size("adapter")
    last = row_n_seq - 2
    pairs = []
    for s in range(peers):
        t = s + last if s % row_n_seq < 2 else s - 2
        pairs += [(s * planes + a, t * planes + a) for a in range(planes)]
    return lax.ppermute(value, both_axes, pairs)


def along_z_back(value):
    peers, planes = lax.axis_size("seq"), lax.axis_size("adapter")
    last = row_n_seq - 2
    pairs = [
        (s * planes + a, (s - row_n_seq) * planes + planes - 1 - a)
        for s in range(row_n_seq, peers)
        if s % row_n_seq >= last
        for a in range(planes)
    ]
    relayed = lax.ppermute(value, both_axes, pairs)
    return jnp.where(lax.axis_index("seq") % row_n_seq >= last, relayed, value)


def grouped(value, groups):
    return lax.all_to_all(value, "seq", 0, 0, axis_index_groups=groups, tiled=True)


def fold(x, op):
    return op(x.reshape(x.shape[0] // 8, 8, x.shape[1]), axis=0)


def chunks(stretch, chunk):
    for d in range(3):
        for c in range(0, stretch, chunk):
            yield d, slice(c, c + chunk), slice(d * stretch + c, d * stretch + c + chunk)


def attention_kernel(
    where_ref, rel_ref, base_ref, grad_ref, low_ref, up_ref, up_whole_ref, own_in, mid_k_in, mid_v_in, far_in, swap_k_in, swap_v_in, hidden_in,
    own_ref, mid_ref, far_ref, swap_ref, keep_ref, send_ref,
    window_k, window_v, key_t, score, dprob, dscore_low, acc_k, acc_v, hidden, dquery, pieces, block_sems, hidden_sem,
    *, stretch, chunk, rows, adapters, head_dim, heads, per_step, rank, chips, outer,
):
    step = pl.program_id(0)
    factor = head_dim**-0.5
    shift = factor * log2_e
    wide = rows * adapters
    block = where_ref[0]
    odd = lax.rem(block, 2)
    far_slot = 3 - 2 * odd
    swap_slot = 1 + 2 * odd

    def fills():
        sources = (
            (0, own_in.at[0], own_in.at[1]),
            (2, mid_k_in, mid_v_in),
            (far_slot, far_in.at[0], far_in.at[1]),
            (swap_slot, swap_k_in, swap_v_in),
        )
        for i, (slot, source_k, source_v) in enumerate(sources):
            yield pltpu.make_async_copy(source_k, window_k.at[slot], block_sems.at[2 * i])
            yield pltpu.make_async_copy(source_v, window_v.at[slot], block_sems.at[2 * i + 1])

    hidden_copy = pltpu.make_async_copy(hidden_in, hidden, hidden_sem)

    @pl.when(step == 0)
    def _():
        for copy in fills():
            copy.start()
        hidden_copy.start()
        acc_k[...] = jnp.zeros_like(acc_k)
        acc_v[...] = jnp.zeros_like(acc_v)
        for copy in fills():
            copy.wait()
        for d in range(4):
            key_t[:, d * stretch : (d + 1) * stretch] = window_k[d].T

    rel = rel_ref[...]
    place = lax.broadcasted_iota(jnp.int32, (chunk, wide), 0)
    line = block * rows + lax.broadcasted_iota(jnp.int32, (rows, head_dim), 0)
    bias3 = jnp.where(block >= 3, 0.0, masked_score)

    def scores_of(j):
        cols = slice(j * head_dim, (j + 1) * head_dim)
        query_list = []
        grad_list = []
        for a in range(adapters):
            raised = dot(low_ref[a], up_ref[a, :, cols], NN)
            query_list.append(
                (base_ref[a, :, cols].astype(jnp.float32) + adapter_scale * raised).astype(jnp.bfloat16)
            )
            live = line < where_ref[1 + a]
            grad_list.append(
                jnp.where(live, grad_ref[a, :, cols].astype(jnp.float32), 0.0).astype(jnp.bfloat16)
            )
        query = jnp.concatenate(query_list, axis=0)
        grad = jnp.concatenate(grad_list, axis=0)
        highs = [None] * 3
        for d, part, at in chunks(stretch, chunk):
            s = dot(window_k[d, part, :], query, NT)
            dp = dot(window_v[d, part, :], grad, NT)
            if d == 0:
                early = rel >= place + part.start
                s = jnp.where(early, s, dot(window_k[3, part, :], query, NT) + bias3)
                dp = jnp.where(early, dp, dot(window_v[3, part, :], grad, NT))
            score[j, at, :] = s
            dprob[j, at, :] = dp
            top = fold(s, jnp.max)
            highs[d] = top if highs[d] is None else jnp.maximum(highs[d], top)
        peak = highs[0]
        for d in (1, 2):
            peak = jnp.maximum(peak, jnp.where(block >= d, highs[d], masked_score))
        return query, grad, jnp.max(peak, axis=0, keepdims=True)

    def sums_of(j, query, grad, peak):
        levels = [peak] + [jnp.where(block >= d, peak, -masked_score) for d in (1, 2)]
        total = jnp.zeros((8, wide), jnp.float32)
        delta = jnp.zeros((8, wide), jnp.float32)
        for d, part, at in chunks(stretch, chunk):
            e = jnp.exp2((score[j, at, :] - levels[d]) * shift)
            score[j, at, :] = e
            total = total + fold(e, jnp.sum)
            delta = delta + fold(e * dprob[j, at, :], jnp.sum)
        scale = 1.0 / jnp.sum(total, axis=0, keepdims=True)
        return query, grad, scale, jnp.sum(delta, axis=0, keepdims=True) * scale

    def grads_of(j, query, grad, scale, delta):
        for d, part, at in chunks(stretch, chunk):
            p = score[j, at, :] * scale
            ds = p * (dprob[j, at, :] - delta)
            if d == 0:
                early = rel >= place + part.start
                zero = jnp.zeros_like(p)
                split = (
                    (0, jnp.where(early, p, zero), jnp.where(early, ds, zero)),
                    (3, jnp.where(early, zero, p), jnp.where(early, zero, ds)),
                )
            else:
                split = ((d, p, ds),)
            for e, p_e, ds_e in split:
                ds_e = ds_e.astype(jnp.bfloat16)
                dscore_low[j, e * stretch + part.start : e * stretch + part.stop, :] = ds_e
                acc_k[e, part, :] += dot(ds_e, query, NN)
                acc_v[e, part, :] += dot(p_e.astype(jnp.bfloat16), grad, NN)
        part = (dot(key_t[...], dscore_low[j], NN).T * factor).astype(jnp.bfloat16)
        for a in range(adapters):
            dquery[step * per_step + j, a] = part[a * rows : (a + 1) * rows]

    states = [scores_of(j) for j in range(per_step)]
    for j in range(per_step):
        grads_of(j, *sums_of(j, *states[j]))

    @pl.when(step == heads // per_step - 1)
    def _():
        def put(out, slot):
            out[0] = (acc_k[slot] * factor).astype(out.dtype)
            out[1] = acc_v[slot].astype(out.dtype)

        put(own_ref, 0)
        put(mid_ref, 2)
        put(far_ref, far_slot)
        put(swap_ref, swap_slot)
        hidden_copy.wait()
        span = 2 * chips * head_dim
        for a in range(adapters):
            at = slice(a * rank, (a + 1) * rank)
            low_t = low_ref[a].astype(jnp.float32).T.astype(jnp.bfloat16)
            small = jnp.zeros((rank, rows), jnp.float32)
            for h in range(heads):
                mine = dquery[h, a]
                small += dot(up_whole_ref[a, :, h * head_dim : (h + 1) * head_dim], mine, NT)
                pieces[h // chips, chips * outer + h % chips, at, :] = adapter_scale * dot(
                    low_t, mine, NN
                )
            small_low = small.astype(jnp.bfloat16)
            for g in range(outer):
                piece = dot(small_low, hidden[a, :, g * span : (g + 1) * span], NN) * adapter_scale
                for i in range(2 * chips):
                    pieces[i % 2, (i // 2) * outer + g, at, :] = piece[
                        :, i * head_dim : (i + 1) * head_dim
                    ]
        keep_ref[...] = pieces[odd]
        send_ref[...] = pieces[1 - odd].astype(send_ref.dtype)


def whole(*shape):
    return pl.BlockSpec(shape, lambda h, w: (0,) * len(shape))


def attention_grads(where, rel, base, grad, low, up, own, mids, far, swaps, hidden, chips, outer):
    adapters, rows, features = base.shape
    _, stretch, head_dim = own.shape
    heads = features // head_dim
    rank, wide, width = low.shape[2], rows * adapters, hidden.shape[2]
    per_step = 2
    assert heads == 2 * chips and width == 2 * chips * outer * head_dim
    body = functools.partial(
        attention_kernel,
        stretch=stretch,
        chunk=384,
        rows=rows,
        adapters=adapters,
        head_dim=head_dim,
        heads=heads,
        per_step=per_step,
        rank=rank,
        chips=chips,
        outer=outer,
    )
    per_head = pl.BlockSpec((adapters, rows, per_step * head_dim), lambda h, w: (0, 0, h))
    anywhere = pl.BlockSpec(memory_space=pltpu.HBM)
    blocks = (chips * outer + chips, adapters * rank, head_dim)
    pair = (2, stretch, head_dim)
    return pl.pallas_call(
        body,
        grid_spec=pltpu.PrefetchScalarGridSpec(
            num_scalar_prefetch=1,
            grid=(heads // per_step,),
            in_specs=[
                whole(1, wide),
                per_head,
                per_head,
                whole(adapters, rows, rank),
                pl.BlockSpec((adapters, rank, per_step * head_dim), lambda h, w: (0, 0, h)),
                whole(adapters, rank, features),
            ]
            + [anywhere] * 7,
            out_specs=[whole(*pair)] * 4 + [whole(*blocks)] * 2,
            scratch_shapes=[
                pltpu.VMEM((4, stretch, head_dim), jnp.bfloat16),
                pltpu.VMEM((4, stretch, head_dim), jnp.bfloat16),
                pltpu.VMEM((head_dim, 4 * stretch), jnp.bfloat16),
                pltpu.VMEM((per_step, 3 * stretch, wide), jnp.float32),
                pltpu.VMEM((per_step, 3 * stretch, wide), jnp.float32),
                pltpu.VMEM((per_step, 4 * stretch, wide), jnp.bfloat16),
                pltpu.VMEM((4, stretch, head_dim), jnp.float32),
                pltpu.VMEM((4, stretch, head_dim), jnp.float32),
                pltpu.VMEM((adapters, rows, width), jnp.bfloat16),
                pltpu.VMEM((heads, adapters, rows, head_dim), jnp.bfloat16),
                pltpu.VMEM((2,) + blocks, jnp.float32),
                pltpu.SemaphoreType.DMA((8,)),
                pltpu.SemaphoreType.DMA,
            ],
        ),
        out_shape=[
            jax.ShapeDtypeStruct(pair, kind)
            for kind in (jnp.float32, jnp.float32, jnp.bfloat16, jnp.bfloat16)
        ]
        + [jax.ShapeDtypeStruct(blocks, jnp.float32), jax.ShapeDtypeStruct(blocks, jnp.bfloat16)],
        compiler_params=pltpu.CompilerParams(
            dimension_semantics=("arbitrary",), vmem_limit_bytes=58 * 1024 * 1024
        ),
        name="attention_grads",
    )(where, rel, base, grad, low, up, up, own, *mids, far, *swaps, hidden)


def local(
    hidden,
    response_base_queries,
    attention_output_gradient,
    keys,
    values,
    adapter_down_weight,
    adapter_up_weight,
    lengths,
    offsets,
):
    adapt_n, row_n, feature_n = response_base_queries.shape
    rank = adapter_down_weight.shape[1]
    stretch_n, head_dim = keys.shape
    seq_index = lax.axis_index("seq")
    odd = seq_index % 2 == 1
    planes = lax.axis_size("adapter")
    chips = row_n_seq // 2
    outer = lax.axis_size("seq") // row_n_seq

    own = jnp.stack([keys, values])
    far = moved(own, 1, 3)
    mid_k, mid_v = moved(keys, 2, 2), moved_two_ahead(values)
    low = jnp.einsum(
        "tbu,tyu->tby", hidden, adapter_down_weight, preferred_element_type=jnp.float32
    ).astype(jnp.bfloat16)
    where = jnp.concatenate([seq_index[None].astype(jnp.int32), lengths])
    rel = (offsets - seq_index * stretch_n).reshape(1, adapt_n * row_n)
    mid_k, low, where, rel = lax.optimization_barrier((mid_k, low, where, rel))
    swap_k, swap_v = moved(mid_k, 1, -1), moved(mid_v, 1, -1)
    own_part, mid_part, far_part, swap_part, keep, send = attention_grads(
        where,
        rel,
        response_base_queries,
        attention_output_gradient,
        low,
        adapter_up_weight,
        own,
        (mid_k, mid_v),
        far,
        (swap_k, swap_v),
        hidden,
        chips,
        outer,
    )
    far_back = moved(far_part, -3, -1)
    swap_back = moved(swap_part, 1, -1)
    mid_dk = (mid_part[0] + swap_back[0].astype(jnp.float32)).astype(jnp.bfloat16)
    mid_dv = (mid_part[1] + swap_back[1].astype(jnp.float32)).astype(jnp.bfloat16)
    mid_dv = round_x_back(mid_dv)
    mid_dk = moved(mid_dk, -2, -2)

    n_down = chips * outer
    lanes = keep.shape[2]
    at_core = keep + moved(send, 1, -1).astype(jnp.float32)
    at_core = at_core.astype(jnp.bfloat16)
    up_copies = jnp.broadcast_to(at_core[None, n_down:], (chips, chips) + at_core.shape[1:])
    at_core = jnp.concatenate(
        [at_core[:n_down].reshape(chips, outer, adapt_n * rank, lanes), up_copies], axis=1
    )
    along_x = [[(g * chips + x) * 2 + c for x in range(chips)] for g in range(outer) for c in range(2)]
    at_chip = grouped(at_core, along_x)
    at_chip, far_back, mid_dv = lax.optimization_barrier((at_chip, far_back, mid_dv))
    mid_back = jnp.stack([mid_dk, along_z_back(mid_dv)])
    at_chip = at_chip.astype(jnp.float32).sum(0).astype(jnp.bfloat16)
    up_copies = jnp.broadcast_to(at_chip[None, outer:], (outer, chips) + at_chip.shape[1:])
    at_chip = jnp.concatenate([at_chip[:outer, None], up_copies], axis=1)
    across = [[g * row_n_seq + i for g in range(outer)] for i in range(row_n_seq)]
    summed = grouped(at_chip, across)
    prompt = own_part + far_back.astype(jnp.float32) + mid_back.astype(jnp.float32)
    prompt = prompt.reshape(2, planes, stretch_n // planes, head_dim)
    plane = lax.axis_index("adapter")
    total = lax.dynamic_index_in_dim(prompt, plane, 1, False)
    shares = []
    for other in range(1, planes):
        share = lax.dynamic_index_in_dim(prompt, plane ^ other, 1, False).astype(jnp.bfloat16)
        shares.append(lax.ppermute(share, "adapter", [(a, a ^ other) for a in range(planes)]))
    summed, shares = lax.optimization_barrier((summed, shares))
    prompt = total + sum(share.astype(jnp.float32) for share in shares)
    summed = summed.astype(jnp.float32).sum(0)

    down = summed[0].reshape(adapt_n, rank, lanes)
    up_mine = summed[1:]
    up_other = moved(up_mine, 1, -1)
    up_blocks = jnp.concatenate(
        [jnp.where(odd, up_other, up_mine), jnp.where(odd, up_mine, up_other)], axis=0
    )
    up_blocks = up_blocks.reshape(2 * chips, adapt_n, rank, lanes).transpose(1, 2, 0, 3)
    return (
        down,
        up_blocks.reshape(adapt_n, rank, feature_n),
        prompt[0],
        prompt[1],
    )


def solution(mesh):
    return jax.shard_map(
        local,
        mesh=mesh,
        in_specs=(
            P("adapter", "seq", None),
            P("adapter", "seq", None),
            P("adapter", "seq", None),
            P("seq", None),
            P("seq", None),
            P("adapter", None, None),
            P("adapter", None, None),
            P("adapter"),
            P("adapter", "seq"),
        ),
        out_specs=(
            P("adapter", None, "seq"),
            P("adapter", None, None),
            P(("seq", "adapter"), None),
            P(("seq", "adapter"), None),
        ),
        check_vma=False,
    )
```

```python
import functools

import jax
import jax.numpy as jnp
from jax import lax
from jax.experimental import pallas as pl
from jax.experimental.pallas import tpu as pltpu
from jax.sharding import PartitionSpec as P

adapter_scale = 2.0
masked_score = -1.0e30
log2_e = 1.4426950408889634
both_axes = ("seq", "adapter")
row_n_seq = 8

NN = ((1,), (0,))
NT = ((1,), (1,))


def dot(a, b, dims):
    return lax.dot_general(a, b, (dims, ((), ())), preferred_element_type=jnp.float32)


def moved(value, by_even, by_odd):
    peers, planes = lax.axis_size("seq"), lax.axis_size("adapter")
    pairs = []
    for s in range(peers):
        t = s + (by_odd if s % 2 else by_even)
        if 0 <= t < peers:
            for a in range(planes):
                b = a if t // row_n_seq == s // row_n_seq else planes - 1 - a
                pairs.append((s * planes + a, t * planes + b))
    return lax.ppermute(value, both_axes, pairs)


def moved_two_ahead(value):
    peers, planes = lax.axis_size("seq"), lax.axis_size("adapter")
    last = row_n_seq - 2
    onward, over = [], []
    for s in range(peers):
        t = s - last if s % row_n_seq >= last else s + 2
        for a in range(planes):
            onward.append((s * planes + a, t * planes + a))
            if s % row_n_seq < 2 and s + row_n_seq < peers:
                over.append((s * planes + a, (s + row_n_seq) * planes + planes - 1 - a))
    value = lax.ppermute(value, both_axes, onward)
    relayed = lax.ppermute(value, both_axes, over)
    return jnp.where(lax.axis_index("seq") % row_n_seq < 2, relayed, value)


def round_x_back(value):
    peers, planes = lax.axis_size("seq"), lax.axis_size("adapter")
    last = row_n_seq - 2
    pairs = []
    for s in range(peers):
        t = s + last if s % row_n_seq < 2 else s - 2
        pairs += [(s * planes + a, t * planes + a) for a in range(planes)]
    return lax.ppermute(value, both_axes, pairs)


def along_z_back(value):
    peers, planes = lax.axis_size("seq"), lax.axis_size("adapter")
    last = row_n_seq - 2
    pairs = [
        (s * planes + a, (s - row_n_seq) * planes + planes - 1 - a)
        for s in range(row_n_seq, peers)
        if s % row_n_seq >= last
        for a in range(planes)
    ]
    relayed = lax.ppermute(value, both_axes, pairs)
    return jnp.where(lax.axis_index("seq") % row_n_seq >= last, relayed, value)


def grouped(value, groups):
    return lax.all_to_all(value, "seq", 0, 0, axis_index_groups=groups, tiled=True)


def fold(x, op):
    return op(x.reshape(x.shape[0] // 8, 8, x.shape[1]), axis=0)


def chunks(stretch, chunk):
    for d in range(3):
        for c in range(0, stretch, chunk):
            yield d, slice(c, c + chunk), slice(d * stretch + c, d * stretch + c + chunk)


def attention_kernel(
    where_ref, rel_ref, base_ref, grad_ref, low_ref, up_ref, up_whole_ref, own_in, mid_k_in, mid_v_in, far_in, swap_k_in, swap_v_in, hidden_in,
    own_ref, mid_ref, far_ref, swap_ref, keep_ref, send_ref,
    window_k, window_v, key_t, score, dprob, dscore_low, acc_k, acc_v, hidden, dquery, pieces, block_sems, hidden_sem,
    *, stretch, chunk, rows, adapters, head_dim, heads, per_step, rank, chips, outer,
):
    step = pl.program_id(0)
    factor = head_dim**-0.5
    shift = factor * log2_e
    wide = rows * adapters
    block = where_ref[0]
    odd = lax.rem(block, 2)
    far_slot = 3 - 2 * odd
    swap_slot = 1 + 2 * odd

    def fills():
        sources = (
            (0, own_in.at[0], own_in.at[1]),
            (2, mid_k_in, mid_v_in),
            (far_slot, far_in.at[0], far_in.at[1]),
            (swap_slot, swap_k_in, swap_v_in),
        )
        for i, (slot, source_k, source_v) in enumerate(sources):
            yield pltpu.make_async_copy(source_k, window_k.at[slot], block_sems.at[2 * i])
            yield pltpu.make_async_copy(source_v, window_v.at[slot], block_sems.at[2 * i + 1])

    hidden_copy = pltpu.make_async_copy(hidden_in, hidden, hidden_sem)

    @pl.when(step == 0)
    def _():
        for copy in fills():
            copy.start()
        hidden_copy.start()
        acc_k[...] = jnp.zeros_like(acc_k)
        acc_v[...] = jnp.zeros_like(acc_v)
        for copy in fills():
            copy.wait()
        for d in range(4):
            key_t[:, d * stretch : (d + 1) * stretch] = window_k[d].T

    rel = rel_ref[...]
    place = lax.broadcasted_iota(jnp.int32, (chunk, wide), 0)
    line = block * rows + lax.broadcasted_iota(jnp.int32, (rows, head_dim), 0)
    bias3 = jnp.where(block >= 3, 0.0, masked_score)

    def scores_of(j):
        cols = slice(j * head_dim, (j + 1) * head_dim)
        query_list = []
        grad_list = []
        for a in range(adapters):
            raised = dot(low_ref[a], up_ref[a, :, cols], NN)
            query_list.append(
                (base_ref[a, :, cols].astype(jnp.float32) + adapter_scale * raised).astype(jnp.bfloat16)
            )
            live = line < where_ref[1 + a]
            grad_list.append(
                jnp.where(live, grad_ref[a, :, cols].astype(jnp.float32), 0.0).astype(jnp.bfloat16)
            )
        query = jnp.concatenate(query_list, axis=0)
        grad = jnp.concatenate(grad_list, axis=0)
        highs = [None] * 3
        for d, part, at in chunks(stretch, chunk):
            s = dot(window_k[d, part, :], query, NT)
            dp = dot(window_v[d, part, :], grad, NT)
            if d == 0:
                early = rel >= place + part.start
                s = jnp.where(early, s, dot(window_k[3, part, :], query, NT) + bias3)
                dp = jnp.where(early, dp, dot(window_v[3, part, :], grad, NT))
            score[j, at, :] = s
            dprob[j, at, :] = dp
            top = fold(s, jnp.max)
            highs[d] = top if highs[d] is None else jnp.maximum(highs[d], top)
        peak = highs[0]
        for d in (1, 2):
            peak = jnp.maximum(peak, jnp.where(block >= d, highs[d], masked_score))
        return query, grad, jnp.max(peak, axis=0, keepdims=True)

    def sums_of(j, query, grad, peak):
        levels = [peak] + [jnp.where(block >= d, peak, -masked_score) for d in (1, 2)]
        total = jnp.zeros((8, wide), jnp.float32)
        delta = jnp.zeros((8, wide), jnp.float32)
        for d, part, at in chunks(stretch, chunk):
            e = jnp.exp2((score[j, at, :] - levels[d]) * shift)
            score[j, at, :] = e
            total = total + fold(e, jnp.sum)
            delta = delta + fold(e * dprob[j, at, :], jnp.sum)
        scale = 1.0 / jnp.sum(total, axis=0, keepdims=True)
        return query, grad, scale, jnp.sum(delta, axis=0, keepdims=True) * scale

    def grads_of(j, query, grad, scale, delta):
        for d, part, at in chunks(stretch, chunk):
            p = score[j, at, :] * scale
            ds = (p * (dprob[j, at, :] - delta)).astype(jnp.bfloat16)
            p = p.astype(jnp.bfloat16)
            if d == 0:
                early = jnp.where(rel >= place + part.start, 1.0, 0.0).astype(jnp.bfloat16)
                p_own, ds_own = p * early, ds * early
                split = ((0, p_own, ds_own), (3, p - p_own, ds - ds_own))
            else:
                split = ((d, p, ds),)
            for e, p_e, ds_e in split:
                dscore_low[j, e * stretch + part.start : e * stretch + part.stop, :] = ds_e
                acc_k[e, part, :] += dot(ds_e, query, NN)
                acc_v[e, part, :] += dot(p_e, grad, NN)
        part = (dot(key_t[...], dscore_low[j], NN).T * factor).astype(jnp.bfloat16)
        for a in range(adapters):
            dquery[step * per_step + j, a] = part[a * rows : (a + 1) * rows]

    states = [scores_of(j) for j in range(per_step)]
    for j in range(per_step):
        grads_of(j, *sums_of(j, *states[j]))

    @pl.when(step == heads // per_step - 1)
    def _():
        def put(out, slot):
            out[0] = (acc_k[slot] * factor).astype(out.dtype)
            out[1] = acc_v[slot].astype(out.dtype)

        put(own_ref, 0)
        put(mid_ref, 2)
        put(far_ref, far_slot)
        put(swap_ref, swap_slot)
        hidden_copy.wait()
        span = 2 * chips * head_dim
        for a in range(adapters):
            at = slice(a * rank, (a + 1) * rank)
            low_t = low_ref[a].astype(jnp.float32).T.astype(jnp.bfloat16)
            small = jnp.zeros((rank, rows), jnp.float32)
            for h in range(heads):
                mine = dquery[h, a]
                small += dot(up_whole_ref[a, :, h * head_dim : (h + 1) * head_dim], mine, NT)
                pieces[h // chips, chips * outer + h % chips, at, :] = adapter_scale * dot(
                    low_t, mine, NN
                )
            small_low = small.astype(jnp.bfloat16)
            for g in range(outer):
                piece = dot(small_low, hidden[a, :, g * span : (g + 1) * span], NN) * adapter_scale
                for i in range(2 * chips):
                    pieces[i % 2, (i // 2) * outer + g, at, :] = piece[
                        :, i * head_dim : (i + 1) * head_dim
                    ]
        keep_ref[...] = pieces[odd]
        send_ref[...] = pieces[1 - odd].astype(send_ref.dtype)


def whole(*shape):
    return pl.BlockSpec(shape, lambda h, w: (0,) * len(shape))


def attention_grads(where, rel, base, grad, low, up, own, mids, far, swaps, hidden, chips, outer):
    adapters, rows, features = base.shape
    _, stretch, head_dim = own.shape
    heads = features // head_dim
    rank, wide, width = low.shape[2], rows * adapters, hidden.shape[2]
    per_step = 4
    assert heads == 2 * chips and width == 2 * chips * outer * head_dim
    body = functools.partial(
        attention_kernel,
        stretch=stretch,
        chunk=384,
        rows=rows,
        adapters=adapters,
        head_dim=head_dim,
        heads=heads,
        per_step=per_step,
        rank=rank,
        chips=chips,
        outer=outer,
    )
    per_head = pl.BlockSpec((adapters, rows, per_step * head_dim), lambda h, w: (0, 0, h))
    anywhere = pl.BlockSpec(memory_space=pltpu.HBM)
    blocks = (chips * outer + chips, adapters * rank, head_dim)
    pair = (2, stretch, head_dim)
    return pl.pallas_call(
        body,
        grid_spec=pltpu.PrefetchScalarGridSpec(
            num_scalar_prefetch=1,
            grid=(heads // per_step,),
            in_specs=[
                whole(1, wide),
                per_head,
                per_head,
                whole(adapters, rows, rank),
                pl.BlockSpec((adapters, rank, per_step * head_dim), lambda h, w: (0, 0, h)),
                whole(adapters, rank, features),
            ]
            + [anywhere] * 7,
            out_specs=[whole(*pair)] * 4 + [whole(*blocks)] * 2,
            scratch_shapes=[
                pltpu.VMEM((4, stretch, head_dim), jnp.bfloat16),
                pltpu.VMEM((4, stretch, head_dim), jnp.bfloat16),
                pltpu.VMEM((head_dim, 4 * stretch), jnp.bfloat16),
                pltpu.VMEM((per_step, 3 * stretch, wide), jnp.float32),
                pltpu.VMEM((per_step, 3 * stretch, wide), jnp.float32),
                pltpu.VMEM((per_step, 4 * stretch, wide), jnp.bfloat16),
                pltpu.VMEM((4, stretch, head_dim), jnp.float32),
                pltpu.VMEM((4, stretch, head_dim), jnp.float32),
                pltpu.VMEM((adapters, rows, width), jnp.bfloat16),
                pltpu.VMEM((heads, adapters, rows, head_dim), jnp.bfloat16),
                pltpu.VMEM((2,) + blocks, jnp.float32),
                pltpu.SemaphoreType.DMA((8,)),
                pltpu.SemaphoreType.DMA,
            ],
        ),
        out_shape=[
            jax.ShapeDtypeStruct(pair, kind)
            for kind in (jnp.float32, jnp.float32, jnp.bfloat16, jnp.bfloat16)
        ]
        + [jax.ShapeDtypeStruct(blocks, jnp.float32), jax.ShapeDtypeStruct(blocks, jnp.bfloat16)],
        compiler_params=pltpu.CompilerParams(
            dimension_semantics=("arbitrary",), vmem_limit_bytes=58 * 1024 * 1024
        ),
        name="attention_grads",
    )(where, rel, base, grad, low, up, up, own, *mids, far, *swaps, hidden)


def local(
    hidden,
    response_base_queries,
    attention_output_gradient,
    keys,
    values,
    adapter_down_weight,
    adapter_up_weight,
    lengths,
    offsets,
):
    adapt_n, row_n, feature_n = response_base_queries.shape
    rank = adapter_down_weight.shape[1]
    stretch_n, head_dim = keys.shape
    seq_index = lax.axis_index("seq")
    odd = seq_index % 2 == 1
    planes = lax.axis_size("adapter")
    chips = row_n_seq // 2
    outer = lax.axis_size("seq") // row_n_seq

    own = jnp.stack([keys, values])
    far = moved(own, 1, 3)
    mid_k, mid_v = moved(keys, 2, 2), moved_two_ahead(values)
    low = jnp.einsum(
        "tbu,tyu->tby", hidden, adapter_down_weight, preferred_element_type=jnp.float32
    ).astype(jnp.bfloat16)
    where = jnp.concatenate([seq_index[None].astype(jnp.int32), lengths])
    rel = (offsets - seq_index * stretch_n).reshape(1, adapt_n * row_n)
    mid_k, low, where, rel = lax.optimization_barrier((mid_k, low, where, rel))
    swap_k, swap_v = moved(mid_k, 1, -1), moved(mid_v, 1, -1)
    own_part, mid_part, far_part, swap_part, keep, send = attention_grads(
        where,
        rel,
        response_base_queries,
        attention_output_gradient,
        low,
        adapter_up_weight,
        own,
        (mid_k, mid_v),
        far,
        (swap_k, swap_v),
        hidden,
        chips,
        outer,
    )
    far_back = moved(far_part, -3, -1)
    swap_back = moved(swap_part, 1, -1)
    mid_dk = (mid_part[0] + swap_back[0].astype(jnp.float32)).astype(jnp.bfloat16)
    mid_dv = (mid_part[1] + swap_back[1].astype(jnp.float32)).astype(jnp.bfloat16)
    mid_dv = round_x_back(mid_dv)
    mid_dk = moved(mid_dk, -2, -2)

    n_down = chips * outer
    lanes = keep.shape[2]
    at_core = keep + moved(send, 1, -1).astype(jnp.float32)
    at_core = at_core.astype(jnp.bfloat16)
    up_copies = jnp.broadcast_to(at_core[None, n_down:], (chips, chips) + at_core.shape[1:])
    at_core = jnp.concatenate(
        [at_core[:n_down].reshape(chips, outer, adapt_n * rank, lanes), up_copies], axis=1
    )
    along_x = [[(g * chips + x) * 2 + c for x in range(chips)] for g in range(outer) for c in range(2)]
    at_chip = grouped(at_core, along_x)
    at_chip, far_back, mid_dv = lax.optimization_barrier((at_chip, far_back, mid_dv))
    mid_back = jnp.stack([mid_dk, along_z_back(mid_dv)])
    at_chip = at_chip.astype(jnp.float32).sum(0).astype(jnp.bfloat16)
    up_copies = jnp.broadcast_to(at_chip[None, outer:], (outer, chips) + at_chip.shape[1:])
    at_chip = jnp.concatenate([at_chip[:outer, None], up_copies], axis=1)
    across = [[g * row_n_seq + i for g in range(outer)] for i in range(row_n_seq)]
    summed = grouped(at_chip, across)
    prompt = own_part + far_back.astype(jnp.float32) + mid_back.astype(jnp.float32)
    prompt = prompt.reshape(2, planes, stretch_n // planes, head_dim)
    plane = lax.axis_index("adapter")
    total = lax.dynamic_index_in_dim(prompt, plane, 1, False)
    shares = []
    for other in range(1, planes):
        share = lax.dynamic_index_in_dim(prompt, plane ^ other, 1, False).astype(jnp.bfloat16)
        shares.append(lax.ppermute(share, "adapter", [(a, a ^ other) for a in range(planes)]))
    summed, shares = lax.optimization_barrier((summed, shares))
    prompt = total + sum(share.astype(jnp.float32) for share in shares)
    summed = summed.astype(jnp.float32).sum(0)

    down = summed[0].reshape(adapt_n, rank, lanes)
    up_mine = summed[1:]
    up_other = moved(up_mine, 1, -1)
    up_blocks = jnp.concatenate(
        [jnp.where(odd, up_other, up_mine), jnp.where(odd, up_mine, up_other)], axis=0
    )
    up_blocks = up_blocks.reshape(2 * chips, adapt_n, rank, lanes).transpose(1, 2, 0, 3)
    return (
        down,
        up_blocks.reshape(adapt_n, rank, feature_n),
        prompt[0],
        prompt[1],
    )


def solution(mesh):
    return jax.shard_map(
        local,
        mesh=mesh,
        in_specs=(
            P("adapter", "seq", None),
            P("adapter", "seq", None),
            P("adapter", "seq", None),
            P("seq", None),
            P("seq", None),
            P("adapter", None, None),
            P("adapter", None, None),
            P("adapter"),
            P("adapter", "seq"),
        ),
        out_specs=(
            P("adapter", None, "seq"),
            P("adapter", None, None),
            P(("seq", "adapter"), None),
            P(("seq", "adapter"), None),
        ),
        check_vma=False,
    )
```
